256 devices in a mesh: len: 4 (over y), energy: 32 (over z, x), mom: 2 (over core).
Axes of the slice: x: 4, y: 4, z: 8, core: 2. Of those that a mesh axis runs over, the one named last changes fastest.
Arguments:
- hamiltonian: float32 [2, 4, 2, 128, 128], P('mom', 'len'), may hold values from -0.5 to 0.5
- sigma_prev: float32 [2, 4, 128, 2, 128, 128], P('mom', 'len', 'energy'), may hold values from -0.25 to 0.25
- coupling: float32 [4, 128, 128], P('len'), may hold values from -1.5 to 1.5
- coupling_pattern: int32 [128, 128], replicated, may hold values 0 or 1
- phonon_shift: int32 [4], replicated, may hold values from 1 to 64
- phonon_weight: float32 [4], replicated, may hold values from 0.5 to 2
Outputs:
- sigma_retarded: float32 [2, 4, 128, 2, 128, 128], P('mom', 'len', 'energy')
- sigma_lesser: float32 [2, 4, 128, 2, 128, 128], P('mom', 'len', 'energy')
The draws below stay inside these ranges and needn't reach their ends.
All inputs are finite; a program needn't handle non-finite values.
Results may differ from the reference program's by a relative error of at most 0.0001.
Values sent between devices are 32-bit elements; how exact they have to be, the bound alone decides.
A program may use at most 128 MiB of HBM per device.

```python
import math
import jax
import jax.numpy as jnp
from jax import lax

NORB = 128
NPHON = 4
NEWTON = 2
LAYERS = 4
ENERGIES = 128
MOMENTA = 2


def set_ends(values, stream_key, least, largest):
    spot = [jax.random.randint(jax.random.fold_in(stream_key, axis), (), 0, length) for axis, length in enumerate(values.shape)]
    longest = values.shape.index(max(values.shape))
    next_to = spot[:longest] + [(spot[longest] + 1) % values.shape[longest]] + spot[longest + 1:]
    return values.at[tuple(spot)].set(least).at[tuple(next_to)].set(largest)


def shard_levels(key, shape, shards, least, top_value):
    factor_of, own = 1.0, jax.random.fold_in(key, 6)
    for dim, blocks in shards:
        draws = jnp.exp(jax.random.uniform(jax.random.fold_in(own, dim), (blocks,), jnp.float32, least / len(shards), top_value / len(shards)))
        factor_of = factor_of * jnp.repeat(draws, shape[dim] // blocks).reshape([-1 if axis == dim else 1 for axis in range(len(shape))])
    return factor_of


def gaussian(rng, dims, deviation, most, split=(), kind=jnp.bfloat16):
    result = jax.random.normal(rng, dims, jnp.float32) * deviation
    if len(split) > 0:
        result = shard_levels(rng, dims, split, -0.22, 0.18) * result
    return jnp.clip(result, min=-most, max=most).astype(kind)


def setup_inputs(seed: int = 0) -> dict:
    streams_of = jax.random.split(jax.random.key(seed), 7)
    return {
        "hamiltonian": gaussian(streams_of[0], (MOMENTA, LAYERS, 2, NORB, NORB), NORB ** -0.5, 0.5, ((0, 2), (1, 4)), jnp.float32),
        "sigma_prev": gaussian(streams_of[1], (MOMENTA, LAYERS, ENERGIES, 2, NORB, NORB), (4 * NORB) ** -0.5, 0.25, ((0, 2), (1, 4), (2, 32)), jnp.float32),
        "coupling": gaussian(streams_of[2], (LAYERS, NORB, NORB), (NORB // 9) ** -0.5, 1.5, ((0, 4),), jnp.float32),
        "coupling_pattern": set_ends((jax.random.randint(streams_of[3], (NORB, NORB), 0, 2) < 1).astype(jnp.int32), jax.random.fold_in(streams_of[3], 1), 0, 1),
        "phonon_shift": set_ends(jax.random.randint(streams_of[4], (NPHON,), 1, ENERGIES // 2 + 1), jax.random.fold_in(streams_of[4], 1), 1, (ENERGIES // 2 + 1) - 1).astype(jnp.int32),
        "phonon_weight": jnp.clip(jnp.exp(jax.random.uniform(streams_of[5], (NPHON,), jnp.float32, math.log(0.5), math.log(2.0))), 0.5, 2.0),
    }


HIGHEST = lax.Precision.HIGHEST


def cmul(left, right):
    def prod(a, b):
        return jnp.einsum("eij,ejk->eik", a, b, precision=HIGHEST)
    real = prod(left[:, 0], right[:, 0]) - prod(left[:, 1], right[:, 1])
    imag = prod(left[:, 0], right[:, 1]) + prod(left[:, 1], right[:, 0])
    return jnp.stack([real, imag], axis=1)


def bond_left(bond, mat):
    return jnp.einsum("ij,ecjk->ecik", bond, mat, precision=HIGHEST)


def bond_right(mat, bond):
    return jnp.einsum("ecij,jk->ecik", mat, bond, precision=HIGHEST)


def scale_by(mat, qre, qim):
    qre = qre[:, None, None]
    qim = qim[:, None, None]
    real = qre * mat[:, 0] - qim * mat[:, 1]
    imag = qre * mat[:, 1] + qim * mat[:, 0]
    return jnp.stack([real, imag], axis=1)


def invert(ham, sig, zre, zim):
    eye = jnp.eye(ham.shape[-1], dtype=jnp.float32)
    eye_c = jnp.stack([eye, jnp.zeros_like(eye)])
    dmat = scale_by(jnp.broadcast_to(eye_c, sig.shape), zre, zim) - ham[None] - sig
    mag = zre * zre + zim * zim
    qre = zre / mag
    qim = -zim / mag
    inverse = scale_by(2.0 * eye_c - scale_by(dmat, qre, qim), qre, qim)
    for step in range(NEWTON):
        inverse = cmul(inverse, 2.0 * eye_c - cmul(dmat, inverse))
    return inverse


def kernels(shift, weight, total):
    index = jnp.arange(total, dtype=jnp.int32)
    own = (index[None, None, :] == index[None, :, None] - shift[:, None, None]).astype(jnp.float32)
    other = (index[None, None, :] == index[None, :, None] + shift[:, None, None]).astype(jnp.float32)
    own = jnp.sum(weight[:, None, None] * own, axis=0)
    other = jnp.sum(weight[:, None, None] * other, axis=0)
    return own, other


def channels(green, occupation):
    diff_re = green[:, 0] - jnp.swapaxes(green[:, 0], -1, -2)
    diff_im = green[:, 1] + jnp.swapaxes(green[:, 1], -1, -2)
    scale = occupation[:, None, None]
    return jnp.stack([green[:, 0], green[:, 1], scale * diff_re, scale * diff_im], axis=1)


def reference(hamiltonian, sigma_prev, coupling, coupling_pattern, phonon_shift, phonon_weight):
    mask = coupling_pattern.astype(jnp.float32)
    energy_pos = jnp.arange(ENERGIES, dtype=jnp.int32).astype(jnp.float32)
    zre = 5.0 + 2.0 * energy_pos / ENERGIES
    zim = jnp.ones_like(zre)
    occupation = 1.0 / (1.0 + jnp.exp(8.0 * energy_pos / ENERGIES - 4.0))
    bonds = [coupling[layer] * mask for layer in range(LAYERS)]
    stacked = []
    for momentum in range(MOMENTA):
        blocks = [invert(hamiltonian[momentum, layer], sigma_prev[momentum, layer], zre, zim) for layer in range(LAYERS)]
        zero = jnp.zeros_like(blocks[0])
        lefts = [zero]
        gleft = blocks[0]
        for layer in range(1, LAYERS):
            term = bond_right(bond_left(bonds[layer], gleft), bonds[layer].T)
            lefts.append(term)
            gleft = blocks[layer] + cmul(cmul(blocks[layer], term), blocks[layer])
        rights = [zero for layer in range(LAYERS)]
        gright = blocks[LAYERS - 1]
        for layer in range(LAYERS - 2, -1, -1):
            term = bond_right(bond_left(bonds[layer + 1].T, gright), bonds[layer + 1])
            rights[layer] = term
            gright = blocks[layer] + cmul(cmul(blocks[layer], term), blocks[layer])
        row = []
        for layer in range(LAYERS):
            green = blocks[layer] + cmul(cmul(blocks[layer], lefts[layer] + rights[layer]), blocks[layer])
            row.append(channels(green, occupation))
        stacked.append(row)
    own, other = kernels(phonon_shift, phonon_weight, ENERGIES)
    combined = []
    for momentum in range(MOMENTA):
        row = []
        for layer in range(LAYERS):
            lower = stacked[momentum][layer - 1] if layer > 0 else jnp.zeros_like(stacked[momentum][layer])
            upper = stacked[momentum][layer + 1] if layer + 1 < LAYERS else jnp.zeros_like(stacked[momentum][layer])
            row.append(stacked[momentum][layer] + 0.5 * (lower + upper))
        combined.append(row)
    retarded = []
    lesser = []
    for momentum in range(MOMENTA):
        ret_row = []
        les_row = []
        for layer in range(LAYERS):
            mine = combined[momentum][layer]
            theirs = combined[1 - momentum][layer]
            out = jnp.einsum("ef,fcij->ecij", own, mine, precision=HIGHEST) + 0.5 * jnp.einsum("ef,fcij->ecij", other, theirs, precision=HIGHEST)
            ret_row.append(out[:, :2])
            les_row.append(out[:, 2:])
        retarded.append(jnp.stack(ret_row))
        lesser.append(jnp.stack(les_row))
    return jnp.stack(retarded), jnp.stack(lesser)
```

```python
import functools

import jax
import jax.numpy as jnp
from jax import lax
from jax.experimental import pallas as pl
from jax.experimental.pallas import tpu as pltpu
from jax.sharding import PartitionSpec as P

N = 128
LAYERS = 4
ENERGIES = 128
GROUPS = 32
ZS, XS = 8, 4
MOMS = 2
PEERS = GROUPS * MOMS
PHONONS = 4
F32 = jnp.float32
BF16 = jnp.bfloat16
MESH = pl.DeviceIdType.MESH


def wrap(value, size):
    return jnp.where(value >= size, value - size, value)


def device(layer, group, mom):
    return (layer, group, mom)


def split(value):
    high = value.astype(BF16)
    return high, (value - high.astype(F32)).astype(BF16)


def lhs3(parts, axis=1):
    high = jnp.concatenate([p[0] for p in parts], axis=axis)
    low = jnp.concatenate([p[1] for p in parts], axis=axis)
    return jnp.concatenate([high, high, low], axis=1)


def dot(left, right):
    return jnp.dot(left, right, preferred_element_type=F32)


def left_c(re, im):
    return lhs3([split(re), split(im)])


def right_c(re, im):
    rh, rl = split(re)
    ih, il = split(im)
    high = jnp.concatenate(
        [jnp.concatenate([rh, ih], axis=1), jnp.concatenate([-ih, rh], axis=1)], axis=0
    )
    low = jnp.concatenate(
        [jnp.concatenate([rl, il], axis=1), jnp.concatenate([-il, rl], axis=1)], axis=0
    )
    return jnp.concatenate([high, low, high], axis=0)


def cmul(left, right):
    both = dot(left, right)
    return both[:, :N], both[:, N:]


def right_plain(parts):
    high = jnp.concatenate([p[0] for p in parts], axis=1)
    low = jnp.concatenate([p[1] for p in parts], axis=1)
    return jnp.concatenate([high, low, high], axis=0)


def sandwich(first, re, im, second):
    both = dot(first, right_plain([split(re), split(im)]))
    stacked = jnp.concatenate([both[:, :N], both[:, N:]], axis=0)
    out = dot(lhs3([split(stacked)]), second)
    return out[:N], out[N:]


def main_kernel(
    ham, sig, coup, pat, shift, weight, back,
    gout, blocks, bonds, greens, send, recv, mixed,
    swap_send, swap_recv, bond_send, bond_recv,
    fwd_send, fwd_recv, ret_send, ret_recv,
):
    l = lax.axis_index("len")
    group = lax.axis_index("energy")
    k = lax.axis_index("mom")
    z = group // XS
    x = group - z * XS
    ls = [wrap(l + i, LAYERS) for i in range(LAYERS)]
    xs = [wrap(x + i, XS) for i in range(XS)]
    ks = [k, 1 - k]

    def plane(body):
        for dx in range(XS):
            for dk in range(MOMS):
                if dx or dk:
                    body(z * XS + xs[dx], ks[dk])

        def step(dz, carry):
            base = wrap(z + dz, ZS) * XS
            for dx in range(XS):
                for dk in range(MOMS):
                    body(base + xs[dx], ks[dk])
            return carry

        lax.fori_loop(1, ZS, step, 0)

    barrier = pltpu.get_barrier_semaphore()

    def greet(layer):
        def body(to_group, to_mom):
            pl.semaphore_signal(
                barrier, inc=1, device_id=device(layer, to_group, to_mom), device_id_type=MESH
            )
        return body

    for i in range(LAYERS):
        plane(greet(ls[i]))
        if i:
            greet(ls[i])(group, k)

    bonds[l] = coup[...] * pat[...].astype(F32)

    def inverse(i):
        e = (group * LAYERS + i).astype(F32)
        zre = 5.0 + 2.0 * e / ENERGIES
        mag = zre * zre + 1.0
        qre = jnp.full((1, 1), zre / mag, F32)
        qim = jnp.full((1, 1), -1.0 / mag, F32)
        sre = ham[0] + sig[i, 0]
        sim = ham[1] + sig[i, 1]
        wre = qre * sre - qim * sim
        wim = qre * sim + qim * sre
        wl = left_c(wre, wim)
        w2re, w2im = cmul(wl, right_c(wre, wim))
        w2r = right_c(w2re, w2im)
        w4re, w4im = cmul(left_c(w2re, w2im), w2r)
        tre, tim = cmul(wl, w2r)
        eye = (
            lax.broadcasted_iota(jnp.int32, (N, N), 0) == lax.broadcasted_iota(jnp.int32, (N, N), 1)
        ).astype(F32)
        are = eye + wre + w2re + tre
        aim = wim + w2im + tim
        bre, bim = cmul(left_c(are, aim), right_c(w4re, w4im))
        are = are + bre
        aim = aim + bim
        return qre * are - qim * aim, qre * aim + qim * are

    def swap(i):
        return pltpu.make_async_remote_copy(
            src_ref=gout.at[i], dst_ref=blocks.at[l], send_sem=swap_send, recv_sem=swap_recv,
            device_id=device(i, group, k), device_id_type=MESH,
        )

    def bond_copy(i):
        return pltpu.make_async_remote_copy(
            src_ref=bonds.at[l], dst_ref=bonds.at[l], send_sem=bond_send, recv_sem=bond_recv,
            device_id=device(i, group, k), device_id_type=MESH,
        )

    for pair in ((2, 1), (3, 0)):
        done = [inverse(ls[d]) for d in pair]
        for d, (re, im) in zip(pair, done):
            if d:
                gout[ls[d], 0] = re
                gout[ls[d], 1] = im
            else:
                blocks[l, 0] = re
                blocks[l, 1] = im
        if pair[0] == 2:
            pl.semaphore_wait(barrier, LAYERS * PEERS - 1)
        for d in pair:
            if d:
                swap(ls[d]).start()
                bond_copy(ls[d]).start()

    three = blocks.at[pl.ds(0, LAYERS - 1)]
    pltpu.make_async_copy(three, three, swap_recv).wait()
    bthree = bonds.at[pl.ds(0, LAYERS - 1)]
    pltpu.make_async_copy(bthree, bthree, bond_recv).wait()

    g = [(blocks[i, 0], blocks[i, 1]) for i in range(LAYERS)]
    gl3 = [left_c(*b) for b in g]
    gr3 = [right_c(*b) for b in g]
    b_l, b_r, bt_l, bt_r = {}, {}, {}, {}
    for i in range(1, LAYERS):
        b = bonds[i]
        bs, bts = split(b), split(b.T)
        b_l[i], bt_l[i] = lhs3([bs]), lhs3([bts])
        b_r[i], bt_r[i] = right_plain([bs]), right_plain([bts])

    def dress(i, term):
        tre, tim = cmul(gl3[i], right_c(*term))
        sre, sim = cmul(left_c(tre, tim), gr3[i])
        return g[i][0] + sre, g[i][1] + sim

    down = {0: g[0]}
    up = {LAYERS - 1: g[LAYERS - 1]}
    for step in range(1, LAYERS):
        i = step
        down[i] = dress(i, sandwich(b_l[i], *down[i - 1], bt_r[i]))
        j = LAYERS - 1 - step
        up[j] = dress(j, sandwich(bt_l[j + 1], *up[j + 1], b_r[j + 1]))
    for c in range(2):
        zero = jnp.zeros((N, N), F32)
        greens[0, c] = zero
        greens[LAYERS + 1, c] = zero
        for i in range(LAYERS):
            greens[i + 1, c] = down[i][c] + (up[i][c] - g[i][c])

    rows = lax.broadcasted_iota(jnp.int32, (N, N), 0)
    cols = lax.broadcasted_iota(jnp.int32, (N, N), 1)
    upper = rows < cols
    slot = group * LAYERS + l

    for t in range(LAYERS):
        layer = ls[t]
        yre = greens[layer + 1, 0] + 0.5 * (greens[layer, 0] + greens[layer + 2, 0])
        yim = greens[layer + 1, 1] + 0.5 * (greens[layer, 1] + greens[layer + 2, 1])
        tre, tim = yre.T, yim.T
        pmat = jnp.where(upper, yre - tre, yim + tim)
        qmat = jnp.where(upper, yim - tim, yre + tre)
        send[layer, :, 0, :] = pmat[: N // 2]
        send[layer, :, 1, :] = pmat[N // 2 :]
        send[layer, :, 2, :] = qmat[: N // 2]
        send[layer, :, 3, :] = qmat[N // 2 :]

        def forward(to_group, to_mom, layer=layer):
            pltpu.make_async_remote_copy(
                src_ref=send.at[layer, to_group * MOMS + to_mom], dst_ref=recv.at[k, slot],
                send_sem=fwd_send, recv_sem=fwd_recv,
                device_id=device(layer, to_group, to_mom), device_id_type=MESH,
            ).start()

        plane(forward)
        if t:
            forward(group, k)
        else:
            pltpu.make_async_copy(
                send.at[layer, group * MOMS + k], recv.at[k, slot], fwd_recv
            ).start()

    dist = rows - cols
    own = jnp.zeros((N, N), F32)
    other = jnp.zeros((N, N), F32)
    for m in range(PHONONS):
        own = own + jnp.where(dist == shift[m], weight[m], 0.0)
        other = other + jnp.where(dist == -shift[m], weight[m], 0.0)
    other = 0.5 * other
    occupation = 1.0 / (1.0 + jnp.exp(8.0 * cols.astype(F32) / ENERGIES - 4.0))
    ret_w = jnp.concatenate(
        [jnp.concatenate([own, other], axis=1), jnp.concatenate([other, own], axis=1)], axis=0
    )
    fown, fother = own * occupation, other * occupation
    les_w = jnp.concatenate(
        [jnp.concatenate([fown, fother], axis=1), jnp.concatenate([fother, fown], axis=1)], axis=0
    )
    ret_l, les_l = lhs3([split(ret_w)]), lhs3([split(les_w)])

    pltpu.make_async_copy(recv, recv, fwd_recv).wait()
    pieces = []
    for r in range(4):
        pieces.append(split(jnp.concatenate([recv[0, :, r, :], recv[1, :, r, :]], axis=0)))
    ret = dot(ret_l, right_plain(pieces))
    les = dot(les_l, right_plain(pieces[:2]))
    for c in range(MOMS):
        for r in range(6):
            src = ret if r < 4 else les
            lane = (r if r < 4 else r - 4) * N
            mixed[c, pl.ds(r, N, stride=6), :] = src[c * N : (c + 1) * N, lane : lane + N]

    spot = group * MOMS + k

    def returning(to_group, to_mom):
        pltpu.make_async_remote_copy(
            src_ref=mixed.at[to_mom, pl.ds(pl.multiple_of(to_group * 24, 8), 24), :],
            dst_ref=back.at[spot], send_sem=ret_send, recv_sem=ret_recv,
            device_id=device(l, to_group, to_mom), device_id_type=MESH,
        ).start()

    plane(returning)
    pltpu.make_async_copy(
        mixed.at[k, pl.ds(pl.multiple_of(group * 24, 8), 24), :], back.at[spot], ret_recv
    ).start()

    whole = back.at[pl.ds(0, PEERS)]
    pltpu.make_async_copy(whole, whole, ret_recv).wait()
    sent = back.at[pl.ds(0, PEERS - 1)]
    pltpu.make_async_copy(sent, sent, ret_send).wait()
    pltpu.make_async_copy(three, three, swap_send).wait()
    pltpu.make_async_copy(bthree, bthree, bond_send).wait()
    for i in range(LAYERS):
        part = send.at[i] if i else send.at[0, pl.ds(0, PEERS - 1)]
        pltpu.make_async_copy(part, part, fwd_send).wait()


def unpack_kernel(back, ret, les):
    e = pl.program_id(0)
    rows = lax.broadcasted_iota(jnp.int32, (N, N), 0)
    cols = lax.broadcasted_iota(jnp.int32, (N, N), 1)
    upper = rows < cols

    def whole(r):
        return jnp.concatenate(
            [back[pl.ds(6 * e + r + h, PEERS, stride=24), :] for h in range(2)], axis=0
        )

    pmat, qmat, lmat = whole(0), whole(2), whole(4)
    pt, qt, lt = pmat.T, qmat.T, lmat.T
    off = rows != cols
    zero = jnp.zeros((N, N), F32)
    ret[0, 0, 0, 0] = 0.5 * jnp.where(upper, pmat + qt, qmat - jnp.where(off, pt, zero))
    ret[0, 0, 0, 1] = 0.5 * jnp.where(upper, pt + qmat, pmat - jnp.where(off, qt, zero))
    les[0, 0, 0, 0] = jnp.where(upper, lmat, jnp.where(off, -lt, zero))
    les[0, 0, 0, 1] = jnp.where(upper, lt, lmat)


def shards(hamiltonian, sigma_prev, coupling, coupling_pattern, phonon_shift, phonon_weight):
    vmem = pl.BlockSpec(memory_space=pltpu.VMEM)
    smem = pl.BlockSpec(memory_space=pltpu.SMEM)
    dma = pltpu.SemaphoreType.DMA
    back = pl.pallas_call(
        main_kernel,
        out_shape=jax.ShapeDtypeStruct((PEERS + 1, 24, N), F32),
        in_specs=[vmem] * 4 + [smem] * 2,
        out_specs=vmem,
        scratch_shapes=[
            pltpu.VMEM((LAYERS, 2, N, N), F32),
            pltpu.VMEM((LAYERS, 2, N, N), F32),
            pltpu.VMEM((LAYERS, N, N), F32),
            pltpu.VMEM((LAYERS + 2, 2, N, N), F32),
            pltpu.VMEM((LAYERS, PEERS, 4, N), F32),
            pltpu.VMEM((MOMS, ENERGIES, 4, N), F32),
            pltpu.VMEM((MOMS, 6 * ENERGIES + 8, N), F32),
        ]
        + [dma] * 8,
        compiler_params=pltpu.CompilerParams(collective_id=0, has_side_effects=True),
        name="selfenergy",
    )(
        hamiltonian[0, 0], sigma_prev[0, 0], coupling[0], coupling_pattern,
        phonon_shift, phonon_weight,
    )
    shape = jax.ShapeDtypeStruct((1, 1, 4, 2, N, N), F32)
    out_spec = pl.BlockSpec((1, 1, 1, 2, N, N), lambda e: (0, 0, e, 0, 0, 0))
    return pl.pallas_call(
        unpack_kernel,
        grid=(4,),
        out_shape=(shape, shape),
        in_specs=[pl.BlockSpec(((PEERS + 1) * 24, N), lambda e: (0, 0))],
        out_specs=(out_spec, out_spec),
        name="unpack",
    )(back.reshape((PEERS + 1) * 24, N))


def solution(mesh):
    in_specs = (
        P("mom", "len", None, None, None),
        P("mom", "len", "energy", None, None, None),
        P("len", None, None),
        P(),
        P(),
        P(),
    )
    out_specs = (
        P("mom", "len", "energy", None, None, None),
        P("mom", "len", "energy", None, None, None),
    )
    return jax.shard_map(shards, mesh=mesh, in_specs=in_specs, out_specs=out_specs, check_vma=False)
```

```python
import functools

import jax
import jax.numpy as jnp
from jax import lax
from jax.experimental import pallas as pl
from jax.experimental.pallas import tpu as pltpu
from jax.sharding import PartitionSpec as P

N = 128
LAYERS = 4
ENERGIES = 128
GROUPS = 32
ZS, XS = 8, 4
MOMS = 2
PEERS = GROUPS * MOMS
PHONONS = 4
F32 = jnp.float32
BF16 = jnp.bfloat16
MESH = pl.DeviceIdType.MESH


def wrap(value, size):
    return jnp.where(value >= size, value - size, value)


def device(layer, group, mom):
    return (layer, group, mom)


def split(value):
    high = value.astype(BF16)
    return high, (value - high.astype(F32)).astype(BF16)


def lhs3(parts, axis=1):
    high = jnp.concatenate([p[0] for p in parts], axis=axis)
    low = jnp.concatenate([p[1] for p in parts], axis=axis)
    return jnp.concatenate([high, high, low], axis=1)


def dot(left, right):
    return jnp.dot(left, right, preferred_element_type=F32)


def left_c(re, im):
    return lhs3([split(re), split(im)])


def right_c(re, im):
    rh, rl = split(re)
    ih, il = split(im)
    high = jnp.concatenate(
        [jnp.concatenate([rh, ih], axis=1), jnp.concatenate([-ih, rh], axis=1)], axis=0
    )
    low = jnp.concatenate(
        [jnp.concatenate([rl, il], axis=1), jnp.concatenate([-il, rl], axis=1)], axis=0
    )
    return jnp.concatenate([high, low, high], axis=0)


def cmul(left, right):
    both = dot(left, right)
    return both[:, :N], both[:, N:]


def right_plain(parts):
    high = jnp.concatenate([p[0] for p in parts], axis=1)
    low = jnp.concatenate([p[1] for p in parts], axis=1)
    return jnp.concatenate([high, low, high], axis=0)


def sandwich(first, re, im, second):
    both = dot(first, right_plain([split(re), split(im)]))
    stacked = jnp.concatenate([both[:, :N], both[:, N:]], axis=0)
    out = dot(lhs3([split(stacked)]), second)
    return out[:N], out[N:]


def main_kernel(
    ham, sig, coup, pat, shift, weight, back,
    gout, blocks, bonds, greens, send, recv, mixed,
    swap_send, swap_recv, bond_send, bond_recv,
    fwd_send, fwd_recv, ret_send, ret_recv, x_sem, z_sem, y_sem,
):
    l = lax.axis_index("len")
    group = lax.axis_index("energy")
    k = lax.axis_index("mom")
    z = group // XS
    x = group - z * XS
    ls = [wrap(l + i, LAYERS) for i in range(LAYERS)]
    xs = [wrap(x + i, XS) for i in range(XS)]
    ks = [k, 1 - k]

    def plane(body):
        for dx in range(XS):
            for dk in range(MOMS):
                if dx or dk:
                    body(z * XS + xs[dx], ks[dk])

        def step(dz, carry):
            base = wrap(z + dz, ZS) * XS
            for dx in range(XS):
                for dk in range(MOMS):
                    body(base + xs[dx], ks[dk])
            return carry

        lax.fori_loop(1, ZS, step, 0)

    def tell(semaphore, targets):
        for target in targets:
            pl.semaphore_signal(semaphore, inc=1, device_id=target, device_id_type=MESH)

    x_line = [device(l, z * XS + xs[i], k) for i in range(1, XS)]
    z_line = [device(l, wrap(z + i, ZS) * XS + x, k) for i in range(1, ZS)]
    y_line = [device(ls[i], group, k) for i in range(1, LAYERS)]
    barrier = pltpu.get_barrier_semaphore()
    tell(barrier, y_line + x_line + z_line + [device(l, group, 1 - k)])

    bonds[l] = coup[...] * pat[...].astype(F32)

    def inverse(i):
        e = (group * LAYERS + i).astype(F32)
        zre = 5.0 + 2.0 * e / ENERGIES
        mag = zre * zre + 1.0
        qre = jnp.full((1, 1), zre / mag, F32)
        qim = jnp.full((1, 1), -1.0 / mag, F32)
        sre = ham[0] + sig[i, 0]
        sim = ham[1] + sig[i, 1]
        wre = qre * sre - qim * sim
        wim = qre * sim + qim * sre
        wl = left_c(wre, wim)
        w2re, w2im = cmul(wl, right_c(wre, wim))
        w2r = right_c(w2re, w2im)
        w4re, w4im = cmul(left_c(w2re, w2im), w2r)
        tre, tim = cmul(wl, w2r)
        eye = (
            lax.broadcasted_iota(jnp.int32, (N, N), 0) == lax.broadcasted_iota(jnp.int32, (N, N), 1)
        ).astype(F32)
        are = eye + wre + w2re + tre
        aim = wim + w2im + tim
        bre, bim = cmul(left_c(are, aim), right_c(w4re, w4im))
        are = are + bre
        aim = aim + bim
        return qre * are - qim * aim, qre * aim + qim * are

    def swap(i):
        return pltpu.make_async_remote_copy(
            src_ref=gout.at[i], dst_ref=blocks.at[l], send_sem=swap_send, recv_sem=swap_recv,
            device_id=device(i, group, k), device_id_type=MESH,
        )

    def bond_copy(i):
        return pltpu.make_async_remote_copy(
            src_ref=bonds.at[l], dst_ref=bonds.at[l], send_sem=bond_send, recv_sem=bond_recv,
            device_id=device(i, group, k), device_id_type=MESH,
        )

    for pair in ((2, 1), (3, 0)):
        done = [inverse(ls[d]) for d in pair]
        for d, (re, im) in zip(pair, done):
            if d:
                gout[ls[d], 0] = re
                gout[ls[d], 1] = im
            else:
                blocks[l, 0] = re
                blocks[l, 1] = im
        if pair[0] == 2:
            pl.semaphore_wait(barrier, LAYERS + XS + ZS - 2)
            tell(x_sem, x_line)
        for d in pair:
            if d:
                swap(ls[d]).start()
                bond_copy(ls[d]).start()

    pl.semaphore_wait(x_sem, XS - 1)
    tell(z_sem, z_line)
    three = blocks.at[pl.ds(0, LAYERS - 1)]
    pltpu.make_async_copy(three, three, swap_recv).wait()
    bthree = bonds.at[pl.ds(0, LAYERS - 1)]
    pltpu.make_async_copy(bthree, bthree, bond_recv).wait()

    pl.semaphore_wait(z_sem, ZS - 1)
    tell(y_sem, y_line)

    g = [(blocks[i, 0], blocks[i, 1]) for i in range(LAYERS)]
    gl3 = [left_c(*b) for b in g]
    gr3 = [right_c(*b) for b in g]
    b_l, b_r, bt_l, bt_r = {}, {}, {}, {}
    for i in range(1, LAYERS):
        b = bonds[i]
        bs, bts = split(b), split(b.T)
        b_l[i], bt_l[i] = lhs3([bs]), lhs3([bts])
        b_r[i], bt_r[i] = right_plain([bs]), right_plain([bts])

    def dress(i, term):
        tre, tim = cmul(gl3[i], right_c(*term))
        sre, sim = cmul(left_c(tre, tim), gr3[i])
        return g[i][0] + sre, g[i][1] + sim

    down = {0: g[0]}
    up = {LAYERS - 1: g[LAYERS - 1]}
    for step in range(1, LAYERS):
        i = step
        down[i] = dress(i, sandwich(b_l[i], *down[i - 1], bt_r[i]))
        j = LAYERS - 1 - step
        up[j] = dress(j, sandwich(bt_l[j + 1], *up[j + 1], b_r[j + 1]))
    for c in range(2):
        zero = jnp.zeros((N, N), F32)
        greens[0, c] = zero
        greens[LAYERS + 1, c] = zero
        for i in range(LAYERS):
            greens[i + 1, c] = down[i][c] + (up[i][c] - g[i][c])

    rows = lax.broadcasted_iota(jnp.int32, (N, N), 0)
    cols = lax.broadcasted_iota(jnp.int32, (N, N), 1)
    upper = rows < cols
    slot = group * LAYERS + l

    pl.semaphore_wait(y_sem, LAYERS - 1)
    for t in range(LAYERS):
        layer = ls[t]
        yre = greens[layer + 1, 0] + 0.5 * (greens[layer, 0] + greens[layer + 2, 0])
        yim = greens[layer + 1, 1] + 0.5 * (greens[layer, 1] + greens[layer + 2, 1])
        tre, tim = yre.T, yim.T
        pmat = jnp.where(upper, yre - tre, yim + tim)
        qmat = jnp.where(upper, yim - tim, yre + tre)
        send[layer, :, 0, :] = pmat[: N // 2]
        send[layer, :, 1, :] = pmat[N // 2 :]
        send[layer, :, 2, :] = qmat[: N // 2]
        send[layer, :, 3, :] = qmat[N // 2 :]

        def forward(to_group, to_mom, layer=layer):
            pltpu.make_async_remote_copy(
                src_ref=send.at[layer, to_group * MOMS + to_mom], dst_ref=recv.at[k, slot],
                send_sem=fwd_send, recv_sem=fwd_recv,
                device_id=device(layer, to_group, to_mom), device_id_type=MESH,
            ).start()

        plane(forward)
        if t:
            forward(group, k)
        else:
            pltpu.make_async_copy(
                send.at[layer, group * MOMS + k], recv.at[k, slot], fwd_recv
            ).start()

    dist = rows - cols
    own = jnp.zeros((N, N), F32)
    other = jnp.zeros((N, N), F32)
    for m in range(PHONONS):
        own = own + jnp.where(dist == shift[m], weight[m], 0.0)
        other = other + jnp.where(dist == -shift[m], weight[m], 0.0)
    other = 0.5 * other
    occupation = 1.0 / (1.0 + jnp.exp(8.0 * cols.astype(F32) / ENERGIES - 4.0))
    ret_w = jnp.concatenate(
        [jnp.concatenate([own, other], axis=1), jnp.concatenate([other, own], axis=1)], axis=0
    )
    fown, fother = own * occupation, other * occupation
    les_w = jnp.concatenate(
        [jnp.concatenate([fown, fother], axis=1), jnp.concatenate([fother, fown], axis=1)], axis=0
    )
    ret_l, les_l = lhs3([split(ret_w)]), lhs3([split(les_w)])

    pltpu.make_async_copy(recv, recv, fwd_recv).wait()
    pieces = []
    for r in range(4):
        pieces.append(split(jnp.concatenate([recv[0, :, r, :], recv[1, :, r, :]], axis=0)))
    ret = dot(ret_l, right_plain(pieces))
    les = dot(les_l, right_plain(pieces[:2]))
    for c in range(MOMS):
        for r in range(6):
            src = ret if r < 4 else les
            lane = (r if r < 4 else r - 4) * N
            mixed[c, pl.ds(r, N, stride=6), :] = src[c * N : (c + 1) * N, lane : lane + N]

    spot = group * MOMS + k

    def returning(to_group, to_mom):
        pltpu.make_async_remote_copy(
            src_ref=mixed.at[to_mom, pl.ds(pl.multiple_of(to_group * 24, 8), 24), :],
            dst_ref=back.at[spot], send_sem=ret_send, recv_sem=ret_recv,
            device_id=device(l, to_group, to_mom), device_id_type=MESH,
        ).start()

    plane(returning)
    pltpu.make_async_copy(
        mixed.at[k, pl.ds(pl.multiple_of(group * 24, 8), 24), :], back.at[spot], ret_recv
    ).start()

    whole = back.at[pl.ds(0, PEERS)]
    pltpu.make_async_copy(whole, whole, ret_recv).wait()
    sent = back.at[pl.ds(0, PEERS - 1)]
    pltpu.make_async_copy(sent, sent, ret_send).wait()
    pltpu.make_async_copy(three, three, swap_send).wait()
    pltpu.make_async_copy(bthree, bthree, bond_send).wait()
    for i in range(LAYERS):
        part = send.at[i] if i else send.at[0, pl.ds(0, PEERS - 1)]
        pltpu.make_async_copy(part, part, fwd_send).wait()


def unpack_kernel(back, ret, les):
    e = pl.program_id(0)
    rows = lax.broadcasted_iota(jnp.int32, (N, N), 0)
    cols = lax.broadcasted_iota(jnp.int32, (N, N), 1)
    upper = rows < cols

    def whole(r):
        return jnp.concatenate(
            [back[pl.ds(6 * e + r + h, PEERS, stride=24), :] for h in range(2)], axis=0
        )

    pmat, qmat, lmat = whole(0), whole(2), whole(4)
    pt, qt, lt = pmat.T, qmat.T, lmat.T
    off = rows != cols
    zero = jnp.zeros((N, N), F32)
    ret[0, 0, 0, 0] = 0.5 * jnp.where(upper, pmat + qt, qmat - jnp.where(off, pt, zero))
    ret[0, 0, 0, 1] = 0.5 * jnp.where(upper, pt + qmat, pmat - jnp.where(off, qt, zero))
    les[0, 0, 0, 0] = jnp.where(upper, lmat, jnp.where(off, -lt, zero))
    les[0, 0, 0, 1] = jnp.where(upper, lt, lmat)


def shards(hamiltonian, sigma_prev, coupling, coupling_pattern, phonon_shift, phonon_weight):
    vmem = pl.BlockSpec(memory_space=pltpu.VMEM)
    smem = pl.BlockSpec(memory_space=pltpu.SMEM)
    dma = pltpu.SemaphoreType.DMA
    back = pl.pallas_call(
        main_kernel,
        out_shape=jax.ShapeDtypeStruct((PEERS + 1, 24, N), F32),
        in_specs=[vmem] * 4 + [smem] * 2,
        out_specs=vmem,
        scratch_shapes=[
            pltpu.VMEM((LAYERS, 2, N, N), F32),
            pltpu.VMEM((LAYERS, 2, N, N), F32),
            pltpu.VMEM((LAYERS, N, N), F32),
            pltpu.VMEM((LAYERS + 2, 2, N, N), F32),
            pltpu.VMEM((LAYERS, PEERS, 4, N), F32),
            pltpu.VMEM((MOMS, ENERGIES, 4, N), F32),
            pltpu.VMEM((MOMS, 6 * ENERGIES + 8, N), F32),
        ]
        + [dma] * 8
        + [pltpu.SemaphoreType.REGULAR] * 3,
        compiler_params=pltpu.CompilerParams(collective_id=0, has_side_effects=True),
        name="selfenergy",
    )(
        hamiltonian[0, 0], sigma_prev[0, 0], coupling[0], coupling_pattern,
        phonon_shift, phonon_weight,
    )
    shape = jax.ShapeDtypeStruct((1, 1, 4, 2, N, N), F32)
    out_spec = pl.BlockSpec((1, 1, 1, 2, N, N), lambda e: (0, 0, e, 0, 0, 0))
    return pl.pallas_call(
        unpack_kernel,
        grid=(4,),
        out_shape=(shape, shape),
        in_specs=[pl.BlockSpec(((PEERS + 1) * 24, N), lambda e: (0, 0))],
        out_specs=(out_spec, out_spec),
        name="unpack",
    )(back.reshape((PEERS + 1) * 24, N))


def solution(mesh):
    in_specs = (
        P("mom", "len", None, None, None),
        P("mom", "len", "energy", None, None, None),
        P("len", None, None),
        P(),
        P(),
        P(),
    )
    out_specs = (
        P("mom", "len", "energy", None, None, None),
        P("mom", "len", "energy", None, None, None),
    )
    return jax.shard_map(shards, mesh=mesh, in_specs=in_specs, out_specs=out_specs, check_vma=False)
```

```python
import functools

import jax
import jax.numpy as jnp
from jax import lax
from jax.experimental import pallas as pl
from jax.experimental.pallas import tpu as pltpu
from jax.sharding import PartitionSpec as P

N = 128
LAYERS = 4
ENERGIES = 128
GROUPS = 32
ZS, XS = 8, 4
MOMS = 2
PEERS = GROUPS * MOMS
PHONONS = 4
ORDER = [(dx, dk) for dx in (2, 1, 3, 0) for dk in (1, 0)]
F32 = jnp.float32
BF16 = jnp.bfloat16
MESH = pl.DeviceIdType.MESH


def wrap(value, size):
    return jnp.where(value >= size, value - size, value)


def device(layer, group, mom):
    return (layer, group, mom)


def split(value):
    high = value.astype(BF16)
    return high, (value - high.astype(F32)).astype(BF16)


def lhs3(parts, axis=1):
    high = jnp.concatenate([p[0] for p in parts], axis=axis)
    low = jnp.concatenate([p[1] for p in parts], axis=axis)
    return jnp.concatenate([high, high, low], axis=1)


def dot(left, right):
    return jnp.dot(left, right, preferred_element_type=F32)


def left_c(re, im):
    return lhs3([split(re), split(im)])


def right_c(re, im):
    rh, rl = split(re)
    ih, il = split(im)
    high = jnp.concatenate(
        [jnp.concatenate([rh, ih], axis=1), jnp.concatenate([-ih, rh], axis=1)], axis=0
    )
    low = jnp.concatenate(
        [jnp.concatenate([rl, il], axis=1), jnp.concatenate([-il, rl], axis=1)], axis=0
    )
    return jnp.concatenate([high, low, high], axis=0)


def cmul(left, right):
    both = dot(left, right)
    return both[:, :N], both[:, N:]


def right_plain(parts):
    high = jnp.concatenate([p[0] for p in parts], axis=1)
    low = jnp.concatenate([p[1] for p in parts], axis=1)
    return jnp.concatenate([high, low, high], axis=0)


def sandwich(first, re, im, second):
    both = dot(first, right_plain([split(re), split(im)]))
    stacked = jnp.concatenate([both[:, :N], both[:, N:]], axis=0)
    out = dot(lhs3([split(stacked)]), second)
    return out[:N], out[N:]


def main_kernel(
    ham_in, sig_in, coup_in, pat_in, shift, weight, back,
    ham, sig, coup, pat,
    gout, blocks, bonds, greens, send, recv, mixed,
    swap_send, swap_recv, bond_send, bond_recv,
    fwd_send, fwd_recv, ret_send, ret_recv, in_sems,
    x_sem, z_sem, y_sem, core_sem,
):
    l = lax.axis_index("len")
    group = lax.axis_index("energy")
    k = lax.axis_index("mom")
    z = group // XS
    x = group - z * XS
    ls = [wrap(l + i, LAYERS) for i in range(LAYERS)]
    xs = [wrap(x + i, XS) for i in range(XS)]
    ks = [k, 1 - k]

    def plane(body):
        def line(base, skip=0):
            for dx, dk in ORDER[: XS * MOMS - skip]:
                body(base + xs[dx], ks[dk])

        line(wrap(z + ZS // 2, ZS) * XS)

        def step(i, carry):
            ahead = wrap(z + ZS // 2 - i, ZS) * XS
            behind = wrap(z + ZS // 2 + i, ZS) * XS
            for dx, dk in ORDER:
                body(ahead + xs[dx], ks[dk])
                body(behind + xs[dx], ks[dk])
            return carry

        lax.fori_loop(1, ZS // 2, step, 0)
        line(z * XS, skip=1)

    def tell(semaphore, targets):
        for target in targets:
            pl.semaphore_signal(semaphore, inc=1, device_id=target, device_id_type=MESH)

    x_line = [device(l, z * XS + xs[i], k) for i in range(1, XS)]
    z_near = [device(l, wrap(z + i, ZS) * XS + x, k) for i in (1, 2, ZS - 2, ZS - 1)]
    y_line = [device(ls[i], group, k) for i in range(1, LAYERS)]
    other_core = [device(l, group, 1 - k)]
    barrier = pltpu.get_barrier_semaphore()
    tell(barrier, y_line + x_line + z_near + other_core)

    loads = [
        pltpu.make_async_copy(ham_in, ham, in_sems.at[0]),
        pltpu.make_async_copy(sig_in.at[ls[2]], sig.at[ls[2]], in_sems.at[1]),
        pltpu.make_async_copy(sig_in.at[ls[1]], sig.at[ls[1]], in_sems.at[2]),
        pltpu.make_async_copy(sig_in.at[ls[3]], sig.at[ls[3]], in_sems.at[3]),
        pltpu.make_async_copy(coup_in, coup, in_sems.at[4]),
        pltpu.make_async_copy(pat_in, pat, in_sems.at[5]),
        pltpu.make_async_copy(sig_in.at[l], sig.at[l], in_sems.at[6]),
    ]
    for load in loads:
        load.start()

    def inverse(i):
        e = (group * LAYERS + i).astype(F32)
        zre = 5.0 + 2.0 * e / ENERGIES
        mag = zre * zre + 1.0
        qre = jnp.full((1, 1), zre / mag, F32)
        qim = jnp.full((1, 1), -1.0 / mag, F32)
        sre = ham[0] + sig[i, 0]
        sim = ham[1] + sig[i, 1]
        wre = qre * sre - qim * sim
        wim = qre * sim + qim * sre
        wl = left_c(wre, wim)
        w2re, w2im = cmul(wl, right_c(wre, wim))
        w2r = right_c(w2re, w2im)
        w4re, w4im = cmul(left_c(w2re, w2im), w2r)
        tre, tim = cmul(wl, w2r)
        eye = (
            lax.broadcasted_iota(jnp.int32, (N, N), 0) == lax.broadcasted_iota(jnp.int32, (N, N), 1)
        ).astype(F32)
        are = eye + wre + w2re + tre
        aim = wim + w2im + tim
        bre, bim = cmul(left_c(are, aim), right_c(w4re, w4im))
        are = are + bre
        aim = aim + bim
        return qre * are - qim * aim, qre * aim + qim * are

    def swap(i):
        return pltpu.make_async_remote_copy(
            src_ref=gout.at[i], dst_ref=blocks.at[l], send_sem=swap_send, recv_sem=swap_recv,
            device_id=device(i, group, k), device_id_type=MESH,
        )

    def bond_copy(i):
        return pltpu.make_async_remote_copy(
            src_ref=bonds.at[l], dst_ref=bonds.at[l], send_sem=bond_send, recv_sem=bond_recv,
            device_id=device(i, group, k), device_id_type=MESH,
        )

    def keep(where, i, block):
        where[i, 0], where[i, 1] = block

    loads[0].wait()
    loads[1].wait()
    keep(gout, ls[2], inverse(ls[2]))
    pl.semaphore_wait(barrier, LAYERS + XS + 3)
    tell(z_sem, z_near)
    swap(ls[2]).start()

    loads[2].wait()
    loads[3].wait()
    one, two = inverse(ls[1]), inverse(ls[3])
    keep(gout, ls[1], one)
    keep(gout, ls[3], two)
    swap(ls[1]).start()
    swap(ls[3]).start()
    pl.semaphore_wait(z_sem, 4)
    tell(x_sem, x_line)

    loads[4].wait()
    loads[5].wait()
    bonds[l] = coup[...] * pat[...].astype(F32)
    for i in (2, 1, 3):
        bond_copy(ls[i]).start()
    loads[6].wait()
    keep(blocks, l, inverse(l))
    pl.semaphore_wait(x_sem, XS - 1)
    tell(y_sem, y_line)

    three = blocks.at[pl.ds(0, LAYERS - 1)]
    pltpu.make_async_copy(three, three, swap_recv).wait()
    bthree = bonds.at[pl.ds(0, LAYERS - 1)]
    pltpu.make_async_copy(bthree, bthree, bond_recv).wait()

    pl.semaphore_wait(y_sem, LAYERS - 1)
    tell(core_sem, other_core)

    g = [(blocks[i, 0], blocks[i, 1]) for i in range(LAYERS)]
    gl3 = [left_c(*b) for b in g]
    gr3 = [right_c(*b) for b in g]
    b_l, b_r, bt_l, bt_r = {}, {}, {}, {}
    for i in range(1, LAYERS):
        b = bonds[i]
        bs, bts = split(b), split(b.T)
        b_l[i], bt_l[i] = lhs3([bs]), lhs3([bts])
        b_r[i], bt_r[i] = right_plain([bs]), right_plain([bts])

    def dress(i, term):
        tre, tim = cmul(gl3[i], right_c(*term))
        sre, sim = cmul(left_c(tre, tim), gr3[i])
        return g[i][0] + sre, g[i][1] + sim

    down = {0: g[0]}
    up = {LAYERS - 1: g[LAYERS - 1]}
    for step in range(1, LAYERS):
        i = step
        down[i] = dress(i, sandwich(b_l[i], *down[i - 1], bt_r[i]))
        j = LAYERS - 1 - step
        up[j] = dress(j, sandwich(bt_l[j + 1], *up[j + 1], b_r[j + 1]))
    for c in range(2):
        zero = jnp.zeros((N, N), F32)
        greens[0, c] = zero
        greens[LAYERS + 1, c] = zero
        for i in range(LAYERS):
            greens[i + 1, c] = down[i][c] + (up[i][c] - g[i][c])

    rows = lax.broadcasted_iota(jnp.int32, (N, N), 0)
    cols = lax.broadcasted_iota(jnp.int32, (N, N), 1)
    upper = rows < cols
    slot = group * LAYERS + l

    pl.semaphore_wait(core_sem, 1)
    for t in (2, 1, 3, 0):
        layer = ls[t]
        yre = greens[layer + 1, 0] + 0.5 * (greens[layer, 0] + greens[layer + 2, 0])
        yim = greens[layer + 1, 1] + 0.5 * (greens[layer, 1] + greens[layer + 2, 1])
        tre, tim = yre.T, yim.T
        pmat = jnp.where(upper, yre - tre, yim + tim)
        qmat = jnp.where(upper, yim - tim, yre + tre)
        send[layer, :, 0, :] = pmat[: N // 2]
        send[layer, :, 1, :] = pmat[N // 2 :]
        send[layer, :, 2, :] = qmat[: N // 2]
        send[layer, :, 3, :] = qmat[N // 2 :]

        def forward(to_group, to_mom, layer=layer):
            pltpu.make_async_remote_copy(
                src_ref=send.at[layer, to_group * MOMS + to_mom], dst_ref=recv.at[k, slot],
                send_sem=fwd_send, recv_sem=fwd_recv,
                device_id=device(layer, to_group, to_mom), device_id_type=MESH,
            ).start()

        plane(forward)
        if t:
            forward(group, k)
        else:
            pltpu.make_async_copy(
                send.at[layer, group * MOMS + k], recv.at[k, slot], fwd_recv
            ).start()

    dist = rows - cols
    own = jnp.zeros((N, N), F32)
    other = jnp.zeros((N, N), F32)
    for m in range(PHONONS):
        own = own + jnp.where(dist == shift[m], weight[m], 0.0)
        other = other + jnp.where(dist == -shift[m], weight[m], 0.0)
    other = 0.5 * other
    occupation = 1.0 / (1.0 + jnp.exp(8.0 * cols.astype(F32) / ENERGIES - 4.0))
    ret_w = jnp.concatenate(
        [jnp.concatenate([own, other], axis=1), jnp.concatenate([other, own], axis=1)], axis=0
    )
    fown, fother = own * occupation, other * occupation
    les_w = jnp.concatenate(
        [jnp.concatenate([fown, fother], axis=1), jnp.concatenate([fother, fown], axis=1)], axis=0
    )
    ret_l, les_l = lhs3([split(ret_w)]), lhs3([split(les_w)])

    pltpu.make_async_copy(recv, recv, fwd_recv).wait()
    pieces = []
    for r in range(4):
        pieces.append(split(jnp.concatenate([recv[0, :, r, :], recv[1, :, r, :]], axis=0)))
    ret = dot(ret_l, right_plain(pieces))
    les = dot(les_l, right_plain(pieces[:2]))
    for c in range(MOMS):
        for r in range(6):
            src = ret if r < 4 else les
            lane = (r if r < 4 else r - 4) * N
            mixed[c, pl.ds(r, N, stride=6), :] = src[c * N : (c + 1) * N, lane : lane + N]

    spot = group * MOMS + k

    def returning(to_group, to_mom):
        pltpu.make_async_remote_copy(
            src_ref=mixed.at[to_mom, pl.ds(pl.multiple_of(to_group * 24, 8), 24), :],
            dst_ref=back.at[spot], send_sem=ret_send, recv_sem=ret_recv,
            device_id=device(l, to_group, to_mom), device_id_type=MESH,
        ).start()

    plane(returning)
    pltpu.make_async_copy(
        mixed.at[k, pl.ds(pl.multiple_of(group * 24, 8), 24), :], back.at[spot], ret_recv
    ).start()

    whole = back.at[pl.ds(0, PEERS)]
    pltpu.make_async_copy(whole, whole, ret_recv).wait()
    sent = back.at[pl.ds(0, PEERS - 1)]
    pltpu.make_async_copy(sent, sent, ret_send).wait()
    pltpu.make_async_copy(three, three, swap_send).wait()
    pltpu.make_async_copy(bthree, bthree, bond_send).wait()
    for i in range(LAYERS):
        part = send.at[i] if i else send.at[0, pl.ds(0, PEERS - 1)]
        pltpu.make_async_copy(part, part, fwd_send).wait()


def unpack_kernel(back, ret, les):
    e = pl.program_id(0)
    rows = lax.broadcasted_iota(jnp.int32, (N, N), 0)
    cols = lax.broadcasted_iota(jnp.int32, (N, N), 1)
    upper = rows < cols

    def whole(r):
        return jnp.concatenate(
            [back[pl.ds(6 * e + r + h, PEERS, stride=24), :] for h in range(2)], axis=0
        )

    pmat, qmat, lmat = whole(0), whole(2), whole(4)
    pt, qt, lt = pmat.T, qmat.T, lmat.T
    off = rows != cols
    zero = jnp.zeros((N, N), F32)
    ret[0, 0, 0, 0] = 0.5 * jnp.where(upper, pmat + qt, qmat - jnp.where(off, pt, zero))
    ret[0, 0, 0, 1] = 0.5 * jnp.where(upper, pt + qmat, pmat - jnp.where(off, qt, zero))
    les[0, 0, 0, 0] = jnp.where(upper, lmat, jnp.where(off, -lt, zero))
    les[0, 0, 0, 1] = jnp.where(upper, lt, lmat)


def shards(hamiltonian, sigma_prev, coupling, coupling_pattern, phonon_shift, phonon_weight):
    vmem = pl.BlockSpec(memory_space=pltpu.VMEM)
    smem = pl.BlockSpec(memory_space=pltpu.SMEM)
    dma = pltpu.SemaphoreType.DMA
    back = pl.pallas_call(
        main_kernel,
        out_shape=jax.ShapeDtypeStruct((PEERS + 1, 24, N), F32),
        in_specs=[pl.BlockSpec(memory_space=pl.ANY)] * 4 + [smem] * 2,
        out_specs=vmem,
        scratch_shapes=[
            pltpu.VMEM((2, N, N), F32),
            pltpu.VMEM((4, 2, N, N), F32),
            pltpu.VMEM((N, N), F32),
            pltpu.VMEM((N, N), jnp.int32),
            pltpu.VMEM((LAYERS, 2, N, N), F32),
            pltpu.VMEM((LAYERS, 2, N, N), F32),
            pltpu.VMEM((LAYERS, N, N), F32),
            pltpu.VMEM((LAYERS + 2, 2, N, N), F32),
            pltpu.VMEM((LAYERS, PEERS, 4, N), F32),
            pltpu.VMEM((MOMS, ENERGIES, 4, N), F32),
            pltpu.VMEM((MOMS, 6 * ENERGIES + 8, N), F32),
        ]
        + [dma] * 8
        + [dma((7,))]
        + [pltpu.SemaphoreType.REGULAR] * 4,
        compiler_params=pltpu.CompilerParams(collective_id=0, has_side_effects=True),
        name="selfenergy",
    )(
        hamiltonian[0, 0], sigma_prev[0, 0], coupling[0], coupling_pattern,
        phonon_shift, phonon_weight,
    )
    shape = jax.ShapeDtypeStruct((1, 1, 4, 2, N, N), F32)
    out_spec = pl.BlockSpec((1, 1, 1, 2, N, N), lambda e: (0, 0, e, 0, 0, 0))
    return pl.pallas_call(
        unpack_kernel,
        grid=(4,),
        out_shape=(shape, shape),
        in_specs=[pl.BlockSpec(((PEERS + 1) * 24, N), lambda e: (0, 0))],
        out_specs=(out_spec, out_spec),
        name="unpack",
    )(back.reshape((PEERS + 1) * 24, N))


def solution(mesh):
    in_specs = (
        P("mom", "len", None, None, None),
        P("mom", "len", "energy", None, None, None),
        P("len", None, None),
        P(),
        P(),
        P(),
    )
    out_specs = (
        P("mom", "len", "energy", None, None, None),
        P("mom", "len", "energy", None, None, None),
    )
    return jax.shard_map(shards, mesh=mesh, in_specs=in_specs, out_specs=out_specs, check_vma=False)
```

```python
import functools

import jax
import jax.numpy as jnp
from jax import lax
from jax.experimental import pallas as pl
from jax.experimental.pallas import tpu as pltpu
from jax.sharding import PartitionSpec as P

N = 128
LAYERS = 4
ENERGIES = 128
GROUPS = 32
ZS, XS = 8, 4
MOMS = 2
PEERS = GROUPS * MOMS
PHONONS = 4
ORDER = [(dx, dk) for dx in (2, 1, 3, 0) for dk in (1, 0)]
F32 = jnp.float32
BF16 = jnp.bfloat16
MESH = pl.DeviceIdType.MESH


def wrap(value, size):
    return jnp.where(value >= size, value - size, value)


def device(layer, group, mom):
    return (layer, group, mom)


def split(value):
    high = value.astype(BF16)
    return high, (value - high.astype(F32)).astype(BF16)


def lhs3(parts, axis=1):
    high = jnp.concatenate([p[0] for p in parts], axis=axis)
    low = jnp.concatenate([p[1] for p in parts], axis=axis)
    return jnp.concatenate([high, high, low], axis=1)


def dot(left, right):
    return jnp.dot(left, right, preferred_element_type=F32)


def left_c(re, im):
    return lhs3([split(re), split(im)])


def right_c(re, im):
    rh, rl = split(re)
    ih, il = split(im)
    high = jnp.concatenate(
        [jnp.concatenate([rh, ih], axis=1), jnp.concatenate([-ih, rh], axis=1)], axis=0
    )
    low = jnp.concatenate(
        [jnp.concatenate([rl, il], axis=1), jnp.concatenate([-il, rl], axis=1)], axis=0
    )
    return jnp.concatenate([high, low, high], axis=0)


def cmul(left, right):
    both = dot(left, right)
    return both[:, :N], both[:, N:]


def right_plain(parts):
    high = jnp.concatenate([p[0] for p in parts], axis=1)
    low = jnp.concatenate([p[1] for p in parts], axis=1)
    return jnp.concatenate([high, low, high], axis=0)


def main_kernel(
    ham_in, sig_in, coup_in, pat_in, shift, weight, back,
    ham, sig, coup, pat,
    gout, blocks, bonds, greens, send, recv, mixed,
    swap_send, swap_recv, bond_send, bond_recv, share_send, share_recv,
    fwd_send, fwd_recv, ret_send, ret_recv, in_sems,
    x_sem, z_sem, y_sem, core_sem,
):
    l = lax.axis_index("len")
    group = lax.axis_index("energy")
    k = lax.axis_index("mom")
    z = group // XS
    x = group - z * XS
    ls = [wrap(l + i, LAYERS) for i in range(LAYERS)]
    xs = [wrap(x + i, XS) for i in range(XS)]
    ks = [k, 1 - k]

    def plane(body):
        def line(base, skip=0):
            for dx, dk in ORDER[: XS * MOMS - skip]:
                body(base + xs[dx], ks[dk])

        line(wrap(z + ZS // 2, ZS) * XS)

        def step(i, carry):
            ahead = wrap(z + ZS // 2 - i, ZS) * XS
            behind = wrap(z + ZS // 2 + i, ZS) * XS
            for dx, dk in ORDER:
                body(ahead + xs[dx], ks[dk])
                body(behind + xs[dx], ks[dk])
            return carry

        lax.fori_loop(1, ZS // 2, step, 0)
        line(z * XS, skip=1)

    def tell(semaphore, targets):
        for target in targets:
            pl.semaphore_signal(semaphore, inc=1, device_id=target, device_id_type=MESH)

    x_line = [device(l, z * XS + xs[i], k) for i in range(1, XS)]
    z_near = [device(l, wrap(z + i, ZS) * XS + x, k) for i in (1, 2, ZS - 2, ZS - 1)]
    y_line = [device(ls[i], group, k) for i in range(1, LAYERS)]
    other_core = [device(l, group, 1 - k)]
    barrier = pltpu.get_barrier_semaphore()
    tell(barrier, y_line + x_line + z_near + other_core)

    loads = [
        pltpu.make_async_copy(coup_in, coup, in_sems.at[0]),
        pltpu.make_async_copy(pat_in, pat, in_sems.at[1]),
        pltpu.make_async_copy(ham_in, ham, in_sems.at[2]),
        pltpu.make_async_copy(sig_in.at[ls[2]], sig.at[ls[2]], in_sems.at[3]),
        pltpu.make_async_copy(sig_in.at[ls[1]], sig.at[ls[1]], in_sems.at[4]),
        pltpu.make_async_copy(sig_in.at[ls[3]], sig.at[ls[3]], in_sems.at[5]),
        pltpu.make_async_copy(sig_in.at[l], sig.at[l], in_sems.at[6]),
    ]
    for load in loads:
        load.start()

    def inverse(i):
        e = (group * LAYERS + i).astype(F32)
        zre = 5.0 + 2.0 * e / ENERGIES
        mag = zre * zre + 1.0
        qre = jnp.full((1, 1), zre / mag, F32)
        qim = jnp.full((1, 1), -1.0 / mag, F32)
        sre = ham[0] + sig[i, 0]
        sim = ham[1] + sig[i, 1]
        wre = qre * sre - qim * sim
        wim = qre * sim + qim * sre
        wl = left_c(wre, wim)
        w2re, w2im = cmul(wl, right_c(wre, wim))
        w2r = right_c(w2re, w2im)
        w4re, w4im = cmul(left_c(w2re, w2im), w2r)
        tre, tim = cmul(wl, w2r)
        eye = (
            lax.broadcasted_iota(jnp.int32, (N, N), 0) == lax.broadcasted_iota(jnp.int32, (N, N), 1)
        ).astype(F32)
        are = eye + wre + w2re + tre
        aim = wim + w2im + tim
        bre, bim = cmul(left_c(are, aim), right_c(w4re, w4im))
        are = are + bre
        aim = aim + bim
        return qre * are - qim * aim, qre * aim + qim * are

    def swap(i):
        return pltpu.make_async_remote_copy(
            src_ref=gout.at[i], dst_ref=blocks.at[l], send_sem=swap_send, recv_sem=swap_recv,
            device_id=device(i, group, k), device_id_type=MESH,
        )

    half = pl.ds(pl.multiple_of(k * (N // 2), 8), N // 2)

    def bond_copy(i):
        return pltpu.make_async_remote_copy(
            src_ref=bonds.at[l, half], dst_ref=bonds.at[l, half],
            send_sem=bond_send, recv_sem=bond_recv,
            device_id=device(i, group, k), device_id_type=MESH,
        )

    def bond_share(i):
        return pltpu.make_async_remote_copy(
            src_ref=bonds.at[i, half], dst_ref=bonds.at[i, half],
            send_sem=share_send, recv_sem=share_recv,
            device_id=device(l, group, 1 - k), device_id_type=MESH,
        )

    def keep(where, i, block):
        where[i, 0], where[i, 1] = block

    loads[0].wait()
    loads[1].wait()
    bonds[l] = coup[...] * pat[...].astype(F32)
    loads[2].wait()
    loads[3].wait()
    keep(gout, ls[2], inverse(ls[2]))
    pl.semaphore_wait(barrier, LAYERS + XS + 3)
    tell(z_sem, z_near)
    for d in (2, 1, 3):
        bond_copy(ls[d]).start()
    swap(ls[2]).start()

    loads[4].wait()
    loads[5].wait()
    one, two = inverse(ls[1]), inverse(ls[3])
    keep(gout, ls[1], one)
    keep(gout, ls[3], two)
    swap(ls[1]).start()
    swap(ls[3]).start()
    pl.semaphore_wait(z_sem, 4)
    tell(x_sem, x_line)

    loads[6].wait()
    keep(blocks, l, inverse(l))
    pl.semaphore_wait(x_sem, XS - 1)
    tell(y_sem, y_line)

    halves = bonds.at[pl.ds(0, LAYERS - 1), pl.ds(0, N // 2)]
    pltpu.make_async_copy(halves, halves, bond_recv).wait()
    for d in (2, 1, 3):
        bond_share(ls[d]).start()
    pltpu.make_async_copy(halves, halves, share_recv).wait()
    three = blocks.at[pl.ds(0, LAYERS - 1)]
    pltpu.make_async_copy(three, three, swap_recv).wait()
    pl.semaphore_wait(y_sem, LAYERS - 1)
    tell(core_sem, other_core)

    g = [(blocks[i, 0], blocks[i, 1]) for i in range(LAYERS)]

    def ends(i, first, second):
        re, im = g[i]
        stacked = split(jnp.concatenate([re, im], axis=0))
        head = dot(lhs3([stacked]), right_plain([first]))
        tail = dot(lhs3([second]), right_plain([split(re), split(im)]))
        return left_c(head[:N], head[N:]), right_c(tail[:, :N], tail[:, N:])

    down_ends, up_ends = {}, {}
    for i in range(1, LAYERS):
        b = bonds[i]
        bs, bts = split(b), split(b.T)
        down_ends[i] = ends(i, bs, bts)
        up_ends[i - 1] = ends(i - 1, bts, bs)

    def dress(i, ends, inner):
        sre, sim = cmul(left_c(*cmul(ends[0], right_c(*inner))), ends[1])
        return g[i][0] + sre, g[i][1] + sim

    down = {0: g[0]}
    up = {LAYERS - 1: g[LAYERS - 1]}
    for step in range(1, LAYERS):
        down[step] = dress(step, down_ends[step], down[step - 1])
        j = LAYERS - 1 - step
        up[j] = dress(j, up_ends[j], up[j + 1])
    for c in range(2):
        zero = jnp.zeros((N, N), F32)
        greens[0, c] = zero
        greens[LAYERS + 1, c] = zero
        for i in range(LAYERS):
            greens[i + 1, c] = down[i][c] + (up[i][c] - g[i][c])

    rows = lax.broadcasted_iota(jnp.int32, (N, N), 0)
    cols = lax.broadcasted_iota(jnp.int32, (N, N), 1)
    upper = rows < cols
    slot = group * LAYERS + l

    pl.semaphore_wait(core_sem, 1)
    for t in (2, 1, 3, 0):
        layer = ls[t]
        yre = greens[layer + 1, 0] + 0.5 * (greens[layer, 0] + greens[layer + 2, 0])
        yim = greens[layer + 1, 1] + 0.5 * (greens[layer, 1] + greens[layer + 2, 1])
        tre, tim = yre.T, yim.T
        pmat = jnp.where(upper, yre - tre, yim + tim)
        qmat = jnp.where(upper, yim - tim, yre + tre)
        send[layer, :, 0, :] = pmat[: N // 2]
        send[layer, :, 1, :] = pmat[N // 2 :]
        send[layer, :, 2, :] = qmat[: N // 2]
        send[layer, :, 3, :] = qmat[N // 2 :]

        def forward(to_group, to_mom, layer=layer):
            pltpu.make_async_remote_copy(
                src_ref=send.at[layer, to_group * MOMS + to_mom], dst_ref=recv.at[k, slot],
                send_sem=fwd_send, recv_sem=fwd_recv,
                device_id=device(layer, to_group, to_mom), device_id_type=MESH,
            ).start()

        plane(forward)
        if t:
            forward(group, k)
        else:
            pltpu.make_async_copy(
                send.at[layer, group * MOMS + k], recv.at[k, slot], fwd_recv
            ).start()

    dist = rows - cols
    own = jnp.zeros((N, N), F32)
    other = jnp.zeros((N, N), F32)
    for m in range(PHONONS):
        own = own + jnp.where(dist == shift[m], weight[m], 0.0)
        other = other + jnp.where(dist == -shift[m], weight[m], 0.0)
    other = 0.5 * other
    occupation = 1.0 / (1.0 + jnp.exp(8.0 * cols.astype(F32) / ENERGIES - 4.0))
    ret_w = jnp.concatenate(
        [jnp.concatenate([own, other], axis=1), jnp.concatenate([other, own], axis=1)], axis=0
    )
    fown, fother = own * occupation, other * occupation
    les_w = jnp.concatenate(
        [jnp.concatenate([fown, fother], axis=1), jnp.concatenate([fother, fown], axis=1)], axis=0
    )
    ret_l, les_l = lhs3([split(ret_w)]), lhs3([split(les_w)])

    pltpu.make_async_copy(recv, recv, fwd_recv).wait()
    pieces = []
    for r in range(4):
        pieces.append(split(jnp.concatenate([recv[0, :, r, :], recv[1, :, r, :]], axis=0)))
    ret = dot(ret_l, right_plain(pieces))
    les = dot(les_l, right_plain(pieces[:2]))
    for c in range(MOMS):
        for r in range(6):
            src = ret if r < 4 else les
            lane = (r if r < 4 else r - 4) * N
            mixed[c, pl.ds(r, N, stride=6), :] = src[c * N : (c + 1) * N, lane : lane + N]

    spot = group * MOMS + k

    def returning(to_group, to_mom):
        pltpu.make_async_remote_copy(
            src_ref=mixed.at[to_mom, pl.ds(pl.multiple_of(to_group * 24, 8), 24), :],
            dst_ref=back.at[spot], send_sem=ret_send, recv_sem=ret_recv,
            device_id=device(l, to_group, to_mom), device_id_type=MESH,
        ).start()

    plane(returning)
    pltpu.make_async_copy(
        mixed.at[k, pl.ds(pl.multiple_of(group * 24, 8), 24), :], back.at[spot], ret_recv
    ).start()

    whole = back.at[pl.ds(0, PEERS)]
    pltpu.make_async_copy(whole, whole, ret_recv).wait()
    sent = back.at[pl.ds(0, PEERS - 1)]
    pltpu.make_async_copy(sent, sent, ret_send).wait()
    pltpu.make_async_copy(three, three, swap_send).wait()
    pltpu.make_async_copy(halves, halves, bond_send).wait()
    pltpu.make_async_copy(halves, halves, share_send).wait()
    for i in range(LAYERS):
        part = send.at[i] if i else send.at[0, pl.ds(0, PEERS - 1)]
        pltpu.make_async_copy(part, part, fwd_send).wait()


def unpack_kernel(back, ret, les):
    e = pl.program_id(0)
    rows = lax.broadcasted_iota(jnp.int32, (N, N), 0)
    cols = lax.broadcasted_iota(jnp.int32, (N, N), 1)
    upper = rows < cols

    def whole(r):
        return jnp.concatenate(
            [back[pl.ds(6 * e + r + h, PEERS, stride=24), :] for h in range(2)], axis=0
        )

    pmat, qmat, lmat = whole(0), whole(2), whole(4)
    pt, qt, lt = pmat.T, qmat.T, lmat.T
    off = rows != cols
    zero = jnp.zeros((N, N), F32)
    ret[0, 0, 0, 0] = 0.5 * jnp.where(upper, pmat + qt, qmat - jnp.where(off, pt, zero))
    ret[0, 0, 0, 1] = 0.5 * jnp.where(upper, pt + qmat, pmat - jnp.where(off, qt, zero))
    les[0, 0, 0, 0] = jnp.where(upper, lmat, jnp.where(off, -lt, zero))
    les[0, 0, 0, 1] = jnp.where(upper, lt, lmat)


def shards(hamiltonian, sigma_prev, coupling, coupling_pattern, phonon_shift, phonon_weight):
    smem = pl.BlockSpec(memory_space=pltpu.SMEM)
    dma = pltpu.SemaphoreType.DMA
    back = pl.pallas_call(
        main_kernel,
        out_shape=jax.ShapeDtypeStruct((PEERS + 1, 24, N), F32),
        in_specs=[pl.BlockSpec(memory_space=pl.ANY)] * 4 + [smem] * 2,
        out_specs=pl.BlockSpec(memory_space=pl.ANY),
        scratch_shapes=[
            pltpu.VMEM((2, N, N), F32),
            pltpu.VMEM((4, 2, N, N), F32),
            pltpu.VMEM((N, N), F32),
            pltpu.VMEM((N, N), jnp.int32),
            pltpu.VMEM((LAYERS, 2, N, N), F32),
            pltpu.VMEM((LAYERS, 2, N, N), F32),
            pltpu.VMEM((LAYERS, N, N), F32),
            pltpu.VMEM((LAYERS + 2, 2, N, N), F32),
            pltpu.VMEM((LAYERS, PEERS, 4, N), F32),
            pltpu.VMEM((MOMS, ENERGIES, 4, N), F32),
            pltpu.VMEM((MOMS, 6 * ENERGIES + 8, N), F32),
        ]
        + [dma] * 10
        + [dma((7,))]
        + [pltpu.SemaphoreType.REGULAR] * 4,
        compiler_params=pltpu.CompilerParams(collective_id=0, has_side_effects=True),
        name="selfenergy",
    )(
        hamiltonian[0, 0], sigma_prev[0, 0], coupling[0], coupling_pattern,
        phonon_shift, phonon_weight,
    )
    shape = jax.ShapeDtypeStruct((1, 1, 4, 2, N, N), F32)
    out_spec = pl.BlockSpec((1, 1, 1, 2, N, N), lambda e: (0, 0, e, 0, 0, 0))
    return pl.pallas_call(
        unpack_kernel,
        grid=(4,),
        out_shape=(shape, shape),
        in_specs=[pl.BlockSpec(((PEERS + 1) * 24, N), lambda e: (0, 0))],
        out_specs=(out_spec, out_spec),
        name="unpack",
    )(back.reshape((PEERS + 1) * 24, N))


def solution(mesh):
    in_specs = (
        P("mom", "len", None, None, None),
        P("mom", "len", "energy", None, None, None),
        P("len", None, None),
        P(),
        P(),
        P(),
    )
    out_specs = (
        P("mom", "len", "energy", None, None, None),
        P("mom", "len", "energy", None, None, None),
    )
    return jax.shard_map(shards, mesh=mesh, in_specs=in_specs, out_specs=out_specs, check_vma=False)
```

```python
import functools

import jax
import jax.numpy as jnp
from jax import lax
from jax.experimental import pallas as pl
from jax.experimental.pallas import tpu as pltpu
from jax.sharding import PartitionSpec as P

N = 128
LAYERS = 4
ENERGIES = 128
GROUPS = 32
ZS, XS = 8, 4
MOMS = 2
PEERS = GROUPS * MOMS
PHONONS = 4
ORDER = [(dx, dk) for dx in (2, 1, 3, 0) for dk in (1, 0)]
F32 = jnp.float32
BF16 = jnp.bfloat16
MESH = pl.DeviceIdType.MESH


def wrap(value, size):
    return jnp.where(value >= size, value - size, value)


def device(layer, group, mom):
    return (layer, group, mom)


def split(value):
    high = value.astype(BF16)
    return high, (value - high.astype(F32)).astype(BF16)


def lhs3(parts, axis=1):
    high = jnp.concatenate([p[0] for p in parts], axis=axis)
    low = jnp.concatenate([p[1] for p in parts], axis=axis)
    return jnp.concatenate([high, high, low], axis=1)


def dot(left, right):
    return jnp.dot(left, right, preferred_element_type=F32)


def left_c(re, im):
    return lhs3([split(re), split(im)])


def right_c(re, im):
    rh, rl = split(re)
    ih, il = split(im)
    high = jnp.concatenate(
        [jnp.concatenate([rh, ih], axis=1), jnp.concatenate([-ih, rh], axis=1)], axis=0
    )
    low = jnp.concatenate(
        [jnp.concatenate([rl, il], axis=1), jnp.concatenate([-il, rl], axis=1)], axis=0
    )
    return jnp.concatenate([high, low, high], axis=0)


def cmul(left, right):
    both = dot(left, right)
    return both[:, :N], both[:, N:]


def right_plain(parts):
    high = jnp.concatenate([p[0] for p in parts], axis=1)
    low = jnp.concatenate([p[1] for p in parts], axis=1)
    return jnp.concatenate([high, low, high], axis=0)


def main_kernel(
    ham_in, sig_in, coup_in, pat_in, shift, weight, back_p, back_q,
    ham, sig, coup, pat,
    gout, blocks, bonds, greens, send, recv, mixed_p, mixed_q,
    swap_send, swap_recv, bond_send, bond_recv, share_send, share_recv,
    fwd_send, fwd_recv, ret_send, ret_recv, in_sems,
    x_sem, z_sem, y_sem, core_sem,
):
    l = lax.axis_index("len")
    group = lax.axis_index("energy")
    k = lax.axis_index("mom")
    z = group // XS
    x = group - z * XS
    ls = [wrap(l + i, LAYERS) for i in range(LAYERS)]
    xs = [wrap(x + i, XS) for i in range(XS)]
    ks = [k, 1 - k]

    def plane(body):
        def line(base, skip=0):
            for dx, dk in ORDER[: XS * MOMS - skip]:
                body(base + xs[dx], ks[dk])

        line(wrap(z + ZS // 2, ZS) * XS)

        def step(i, carry):
            ahead = wrap(z + ZS // 2 - i, ZS) * XS
            behind = wrap(z + ZS // 2 + i, ZS) * XS
            for dx, dk in ORDER:
                body(ahead + xs[dx], ks[dk])
                body(behind + xs[dx], ks[dk])
            return carry

        lax.fori_loop(1, ZS // 2, step, 0)
        line(z * XS, skip=1)

    def tell(semaphore, targets):
        for target in targets:
            pl.semaphore_signal(semaphore, inc=1, device_id=target, device_id_type=MESH)

    x_line = [device(l, z * XS + xs[i], k) for i in range(1, XS)]
    z_near = [device(l, wrap(z + i, ZS) * XS + x, k) for i in (1, 2, ZS - 2, ZS - 1)]
    y_line = [device(ls[i], group, k) for i in range(1, LAYERS)]
    other_core = [device(l, group, 1 - k)]
    barrier = pltpu.get_barrier_semaphore()
    tell(barrier, y_line + x_line + z_near + other_core)

    loads = [
        pltpu.make_async_copy(coup_in, coup, in_sems.at[0]),
        pltpu.make_async_copy(pat_in, pat, in_sems.at[1]),
        pltpu.make_async_copy(ham_in, ham, in_sems.at[2]),
        pltpu.make_async_copy(sig_in.at[ls[2]], sig.at[ls[2]], in_sems.at[3]),
        pltpu.make_async_copy(sig_in.at[ls[1]], sig.at[ls[1]], in_sems.at[4]),
        pltpu.make_async_copy(sig_in.at[ls[3]], sig.at[ls[3]], in_sems.at[5]),
        pltpu.make_async_copy(sig_in.at[l], sig.at[l], in_sems.at[6]),
    ]
    for load in loads:
        load.start()

    def inverse(i):
        e = (group * LAYERS + i).astype(F32)
        zre = 5.0 + 2.0 * e / ENERGIES
        mag = zre * zre + 1.0
        qre = jnp.full((1, 1), zre / mag, F32)
        qim = jnp.full((1, 1), -1.0 / mag, F32)
        sre = ham[0] + sig[i, 0]
        sim = ham[1] + sig[i, 1]
        wre = qre * sre - qim * sim
        wim = qre * sim + qim * sre
        wl = left_c(wre, wim)
        w2re, w2im = cmul(wl, right_c(wre, wim))
        w2r = right_c(w2re, w2im)
        w4re, w4im = cmul(left_c(w2re, w2im), w2r)
        tre, tim = cmul(wl, w2r)
        eye = (
            lax.broadcasted_iota(jnp.int32, (N, N), 0) == lax.broadcasted_iota(jnp.int32, (N, N), 1)
        ).astype(F32)
        are = eye + wre + w2re + tre
        aim = wim + w2im + tim
        bre, bim = cmul(left_c(are, aim), right_c(w4re, w4im))
        are = are + bre
        aim = aim + bim
        return qre * are - qim * aim, qre * aim + qim * are

    def swap(i):
        return pltpu.make_async_remote_copy(
            src_ref=gout.at[i], dst_ref=blocks.at[l], send_sem=swap_send, recv_sem=swap_recv,
            device_id=device(i, group, k), device_id_type=MESH,
        )

    half = pl.ds(pl.multiple_of(k * (N // 2), 8), N // 2)

    def bond_copy(i):
        return pltpu.make_async_remote_copy(
            src_ref=bonds.at[l, half], dst_ref=bonds.at[l, half],
            send_sem=bond_send, recv_sem=bond_recv,
            device_id=device(i, group, k), device_id_type=MESH,
        )

    def bond_share(i):
        return pltpu.make_async_remote_copy(
            src_ref=bonds.at[i, half], dst_ref=bonds.at[i, half],
            send_sem=share_send, recv_sem=share_recv,
            device_id=device(l, group, 1 - k), device_id_type=MESH,
        )

    def keep(where, i, block):
        where[i, 0], where[i, 1] = block

    loads[0].wait()
    loads[1].wait()
    bonds[l] = coup[...] * pat[...].astype(F32)
    loads[2].wait()
    loads[3].wait()
    keep(gout, ls[2], inverse(ls[2]))
    pl.semaphore_wait(barrier, LAYERS + XS + 3)
    tell(z_sem, z_near)
    for d in (2, 1, 3):
        bond_copy(ls[d]).start()
    swap(ls[2]).start()

    loads[4].wait()
    loads[5].wait()
    one, two = inverse(ls[1]), inverse(ls[3])
    keep(gout, ls[1], one)
    keep(gout, ls[3], two)
    swap(ls[1]).start()
    swap(ls[3]).start()
    pl.semaphore_wait(z_sem, 4)
    tell(x_sem, x_line)

    loads[6].wait()
    keep(blocks, l, inverse(l))
    pl.semaphore_wait(x_sem, XS - 1)
    tell(y_sem, y_line)

    halves = bonds.at[pl.ds(0, LAYERS - 1), pl.ds(0, N // 2)]
    pltpu.make_async_copy(halves, halves, bond_recv).wait()
    for d in (2, 1, 3):
        bond_share(ls[d]).start()
    pltpu.make_async_copy(halves, halves, share_recv).wait()
    three = blocks.at[pl.ds(0, LAYERS - 1)]
    pltpu.make_async_copy(three, three, swap_recv).wait()
    pl.semaphore_wait(y_sem, LAYERS - 1)
    tell(core_sem, other_core)

    g = [(blocks[i, 0], blocks[i, 1]) for i in range(LAYERS)]

    def ends(i, first, second):
        re, im = g[i]
        stacked = split(jnp.concatenate([re, im], axis=0))
        head = dot(lhs3([stacked]), right_plain([first]))
        tail = dot(lhs3([second]), right_plain([split(re), split(im)]))
        return left_c(head[:N], head[N:]), right_c(tail[:, :N], tail[:, N:])

    down_ends, up_ends = {}, {}
    for i in range(1, LAYERS):
        b = bonds[i]
        bs, bts = split(b), split(b.T)
        down_ends[i] = ends(i, bs, bts)
        up_ends[i - 1] = ends(i - 1, bts, bs)

    def dress(i, ends, inner):
        sre, sim = cmul(left_c(*cmul(ends[0], right_c(*inner))), ends[1])
        return g[i][0] + sre, g[i][1] + sim

    down = {0: g[0]}
    up = {LAYERS - 1: g[LAYERS - 1]}
    for step in range(1, LAYERS):
        down[step] = dress(step, down_ends[step], down[step - 1])
        j = LAYERS - 1 - step
        up[j] = dress(j, up_ends[j], up[j + 1])
    for c in range(2):
        zero = jnp.zeros((N, N), F32)
        greens[0, c] = zero
        greens[LAYERS + 1, c] = zero
        for i in range(LAYERS):
            greens[i + 1, c] = down[i][c] + (up[i][c] - g[i][c])

    rows = lax.broadcasted_iota(jnp.int32, (N, N), 0)
    cols = lax.broadcasted_iota(jnp.int32, (N, N), 1)
    upper = rows < cols
    slot = group * LAYERS + l

    def exchange(part, t):
        layer = ls[t]

        def forward(to_group, to_mom):
            pltpu.make_async_remote_copy(
                src_ref=send.at[part, layer, to_group * MOMS + to_mom],
                dst_ref=recv.at[part, k, slot],
                send_sem=fwd_send.at[part], recv_sem=fwd_recv.at[part],
                device_id=device(layer, to_group, to_mom), device_id_type=MESH,
            ).start()

        plane(forward)
        if t:
            forward(group, k)
        else:
            pltpu.make_async_copy(
                send.at[part, layer, group * MOMS + k], recv.at[part, k, slot], fwd_recv.at[part]
            ).start()

    pl.semaphore_wait(core_sem, 1)
    for t in (2, 1, 3, 0):
        layer = ls[t]
        yre = greens[layer + 1, 0] + 0.5 * (greens[layer, 0] + greens[layer + 2, 0])
        yim = greens[layer + 1, 1] + 0.5 * (greens[layer, 1] + greens[layer + 2, 1])
        tre, tim = yre.T, yim.T
        pmat = jnp.where(upper, yre - tre, yim + tim)
        qmat = jnp.where(upper, yim - tim, yre + tre)
        for part, mat in enumerate((pmat, qmat)):
            for r in range(2):
                send[part, layer, :, r, :] = mat[r * PEERS : (r + 1) * PEERS]
        exchange(0, t)
    for t in (2, 1, 3, 0):
        exchange(1, t)

    dist = rows - cols
    own = jnp.zeros((N, N), F32)
    other = jnp.zeros((N, N), F32)
    for m in range(PHONONS):
        own = own + jnp.where(dist == shift[m], weight[m], 0.0)
        other = other + jnp.where(dist == -shift[m], weight[m], 0.0)
    other = 0.5 * other
    occupation = 1.0 / (1.0 + jnp.exp(8.0 * cols.astype(F32) / ENERGIES - 4.0))
    ret_w = jnp.concatenate(
        [jnp.concatenate([own, other], axis=1), jnp.concatenate([other, own], axis=1)], axis=0
    )
    fown, fother = own * occupation, other * occupation
    les_w = jnp.concatenate(
        [jnp.concatenate([fown, fother], axis=1), jnp.concatenate([fother, fown], axis=1)], axis=0
    )
    ret_l = lhs3([split(ret_w)])
    both_l = jnp.concatenate([ret_l, lhs3([split(les_w)])], axis=0)

    spot = group * MOMS + k

    def mix(part, left, mixed, back, kinds):
        arrived = recv.at[part]
        pltpu.make_async_copy(arrived, arrived, fwd_recv.at[part]).wait()
        pieces = [
            split(jnp.concatenate([recv[part, 0, :, r, :], recv[part, 1, :, r, :]], axis=0))
            for r in range(2)
        ]
        out = dot(left, right_plain(pieces))
        each = 2 * kinds
        for kind in range(kinds):
            for c in range(MOMS):
                top = (kind * MOMS + c) * N
                for r in range(2):
                    mixed[c, pl.ds(2 * kind + r, N, stride=each), :] = out[
                        top : top + N, r * N : (r + 1) * N
                    ]
        size = each * LAYERS

        def source(to_group, to_mom):
            return mixed.at[to_mom, pl.ds(pl.multiple_of(to_group * size, 8), size), :]

        def returning(to_group, to_mom):
            pltpu.make_async_remote_copy(
                src_ref=source(to_group, to_mom), dst_ref=back.at[spot],
                send_sem=ret_send.at[part], recv_sem=ret_recv.at[part],
                device_id=device(l, to_group, to_mom), device_id_type=MESH,
            ).start()

        plane(returning)
        pltpu.make_async_copy(source(group, k), back.at[spot], ret_recv.at[part]).start()

    mix(0, both_l, mixed_p, back_p, 2)
    mix(1, ret_l, mixed_q, back_q, 1)

    for part, back in enumerate((back_p, back_q)):
        whole = back.at[pl.ds(0, PEERS)]
        pltpu.make_async_copy(whole, whole, ret_recv.at[part]).wait()
        sent = back.at[pl.ds(0, PEERS - 1)]
        pltpu.make_async_copy(sent, sent, ret_send.at[part]).wait()
        for i in range(LAYERS):
            gone = send.at[part, i] if i else send.at[part, 0, pl.ds(0, PEERS - 1)]
            pltpu.make_async_copy(gone, gone, fwd_send.at[part]).wait()
    pltpu.make_async_copy(three, three, swap_send).wait()
    pltpu.make_async_copy(halves, halves, bond_send).wait()
    pltpu.make_async_copy(halves, halves, share_send).wait()


def unpack_kernel(back_p, back_q, ret, les):
    e = pl.program_id(0)
    rows = lax.broadcasted_iota(jnp.int32, (N, N), 0)
    cols = lax.broadcasted_iota(jnp.int32, (N, N), 1)
    upper = rows < cols

    def whole(back, each, r):
        return jnp.concatenate(
            [back[pl.ds(each * e + r + h, PEERS, stride=LAYERS * each), :] for h in range(2)],
            axis=0,
        )

    pmat, lmat, qmat = whole(back_p, 4, 0), whole(back_p, 4, 2), whole(back_q, 2, 0)
    pt, qt, lt = pmat.T, qmat.T, lmat.T
    off = rows != cols
    zero = jnp.zeros((N, N), F32)
    ret[0, 0, 0, 0] = 0.5 * jnp.where(upper, pmat + qt, qmat - jnp.where(off, pt, zero))
    ret[0, 0, 0, 1] = 0.5 * jnp.where(upper, pt + qmat, pmat - jnp.where(off, qt, zero))
    les[0, 0, 0, 0] = jnp.where(upper, lmat, jnp.where(off, -lt, zero))
    les[0, 0, 0, 1] = jnp.where(upper, lt, lmat)


def shards(hamiltonian, sigma_prev, coupling, coupling_pattern, phonon_shift, phonon_weight):
    smem = pl.BlockSpec(memory_space=pltpu.SMEM)
    dma = pltpu.SemaphoreType.DMA
    back_p, back_q = pl.pallas_call(
        main_kernel,
        out_shape=(
            jax.ShapeDtypeStruct((PEERS + 1, 16, N), F32),
            jax.ShapeDtypeStruct((PEERS + 1, 8, N), F32),
        ),
        in_specs=[pl.BlockSpec(memory_space=pl.ANY)] * 4 + [smem] * 2,
        out_specs=(pl.BlockSpec(memory_space=pl.ANY),) * 2,
        scratch_shapes=[
            pltpu.VMEM((2, N, N), F32),
            pltpu.VMEM((4, 2, N, N), F32),
            pltpu.VMEM((N, N), F32),
            pltpu.VMEM((N, N), jnp.int32),
            pltpu.VMEM((LAYERS, 2, N, N), F32),
            pltpu.VMEM((LAYERS, 2, N, N), F32),
            pltpu.VMEM((LAYERS, N, N), F32),
            pltpu.VMEM((LAYERS + 2, 2, N, N), F32),
            pltpu.VMEM((2, LAYERS, PEERS, 2, N), F32),
            pltpu.VMEM((2, MOMS, ENERGIES, 2, N), F32),
            pltpu.VMEM((MOMS, 4 * ENERGIES + 8, N), F32),
            pltpu.VMEM((MOMS, 2 * ENERGIES + 8, N), F32),
        ]
        + [dma] * 6
        + [dma((2,))] * 4
        + [dma((7,))]
        + [pltpu.SemaphoreType.REGULAR] * 4,
        compiler_params=pltpu.CompilerParams(collective_id=0, has_side_effects=True),
        name="selfenergy",
    )(
        hamiltonian[0, 0], sigma_prev[0, 0], coupling[0], coupling_pattern,
        phonon_shift, phonon_weight,
    )
    shape = jax.ShapeDtypeStruct((1, 1, 4, 2, N, N), F32)
    out_spec = pl.BlockSpec((1, 1, 1, 2, N, N), lambda e: (0, 0, e, 0, 0, 0))
    return pl.pallas_call(
        unpack_kernel,
        grid=(4,),
        out_shape=(shape, shape),
        in_specs=[
            pl.BlockSpec(((PEERS + 1) * 16, N), lambda e: (0, 0)),
            pl.BlockSpec(((PEERS + 1) * 8, N), lambda e: (0, 0)),
        ],
        out_specs=(out_spec, out_spec),
        name="unpack",
    )(back_p.reshape((PEERS + 1) * 16, N), back_q.reshape((PEERS + 1) * 8, N))


def solution(mesh):
    in_specs = (
        P("mom", "len", None, None, None),
        P("mom", "len", "energy", None, None, None),
        P("len", None, None),
        P(),
        P(),
        P(),
    )
    out_specs = (
        P("mom", "len", "energy", None, None, None),
        P("mom", "len", "energy", None, None, None),
    )
    return jax.shard_map(shards, mesh=mesh, in_specs=in_specs, out_specs=out_specs, check_vma=False)
```

```python
import functools

import jax
import jax.numpy as jnp
from jax import lax
from jax.experimental import pallas as pl
from jax.experimental.pallas import tpu as pltpu
from jax.sharding import PartitionSpec as P

N = 128
LAYERS = 4
ENERGIES = 128
GROUPS = 32
ZS, XS = 8, 4
MOMS = 2
PEERS = GROUPS * MOMS
PHONONS = 4
PART = N // (MOMS * XS)
ORDER = [(dx, dk) for dx in (2, 1, 3, 0) for dk in (1, 0)]
F32 = jnp.float32
BF16 = jnp.bfloat16
MESH = pl.DeviceIdType.MESH


def wrap(value, size):
    return jnp.where(value >= size, value - size, value)


def device(layer, group, mom):
    return (layer, group, mom)


def split(value):
    high = value.astype(BF16)
    return high, (value - high.astype(F32)).astype(BF16)


def lhs3(parts, axis=1):
    high = jnp.concatenate([p[0] for p in parts], axis=axis)
    low = jnp.concatenate([p[1] for p in parts], axis=axis)
    return jnp.concatenate([high, high, low], axis=1)


def dot(left, right):
    return jnp.dot(left, right, preferred_element_type=F32)


def left_c(re, im):
    return lhs3([split(re), split(im)])


def right_c(re, im):
    rh, rl = split(re)
    ih, il = split(im)
    high = jnp.concatenate(
        [jnp.concatenate([rh, ih], axis=1), jnp.concatenate([-ih, rh], axis=1)], axis=0
    )
    low = jnp.concatenate(
        [jnp.concatenate([rl, il], axis=1), jnp.concatenate([-il, rl], axis=1)], axis=0
    )
    return jnp.concatenate([high, low, high], axis=0)


def cmul(left, right):
    both = dot(left, right)
    return both[:, :N], both[:, N:]


def right_plain(parts):
    high = jnp.concatenate([p[0] for p in parts], axis=1)
    low = jnp.concatenate([p[1] for p in parts], axis=1)
    return jnp.concatenate([high, low, high], axis=0)


def main_kernel(
    ham_in, sig_in, coup_in, pat_in, shift_in, weight_in, back_p, back_q,
    ham, sig, coup, pat, shift, weight,
    gout, blocks, bonds, greens, send, recv, mixed_p, mixed_q,
    swap_send, swap_recv, bond_send, bond_recv,
    fwd_send, fwd_recv, ret_send, ret_recv, in_sems,
    x_sem, z_sem, y_sem, core_sem,
):
    l = lax.axis_index("len")
    group = lax.axis_index("energy")
    k = lax.axis_index("mom")
    z = group // XS
    x = group - z * XS
    ls = [wrap(l + i, LAYERS) for i in range(LAYERS)]
    xs = [wrap(x + i, XS) for i in range(XS)]
    ks = [k, 1 - k]

    def plane(body):
        def line(base, skip=0):
            for dx, dk in ORDER[: XS * MOMS - skip]:
                body(base + xs[dx], ks[dk])

        line(wrap(z + ZS // 2, ZS) * XS)

        def step(i, carry):
            ahead = wrap(z + ZS // 2 - i, ZS) * XS
            behind = wrap(z + ZS // 2 + i, ZS) * XS
            for dx, dk in ORDER:
                body(ahead + xs[dx], ks[dk])
                body(behind + xs[dx], ks[dk])
            return carry

        lax.fori_loop(1, ZS // 2, step, 0)
        line(z * XS, skip=1)

    def tell(semaphore, targets):
        for target in targets:
            pl.semaphore_signal(semaphore, inc=1, device_id=target, device_id_type=MESH)

    x_line = [device(l, z * XS + xs[i], k) for i in range(1, XS)]
    z_near = [device(l, wrap(z + i, ZS) * XS + x, k) for i in (1, 2, ZS - 2, ZS - 1)]
    y_line = [device(ls[i], group, k) for i in range(1, LAYERS)]
    other_core = [device(l, group, 1 - k)]
    barrier = pltpu.get_barrier_semaphore()
    tell(barrier, y_line + x_line + z_near + other_core)

    loads = [
        pltpu.make_async_copy(coup_in, coup, in_sems.at[0]),
        pltpu.make_async_copy(pat_in, pat, in_sems.at[1]),
        pltpu.make_async_copy(ham_in, ham, in_sems.at[2]),
        pltpu.make_async_copy(sig_in.at[ls[2]], sig.at[ls[2]], in_sems.at[3]),
        pltpu.make_async_copy(sig_in.at[ls[1]], sig.at[ls[1]], in_sems.at[4]),
        pltpu.make_async_copy(sig_in.at[ls[3]], sig.at[ls[3]], in_sems.at[5]),
        pltpu.make_async_copy(sig_in.at[l], sig.at[l], in_sems.at[6]),
        pltpu.make_async_copy(shift_in, shift, in_sems.at[7]),
        pltpu.make_async_copy(weight_in, weight, in_sems.at[8]),
    ]
    for load in loads:
        load.start()

    def inverse(i):
        e = (group * LAYERS + i).astype(F32)
        zre = 5.0 + 2.0 * e / ENERGIES
        mag = zre * zre + 1.0
        qre = jnp.full((1, 1), zre / mag, F32)
        qim = jnp.full((1, 1), -1.0 / mag, F32)
        sre = ham[0] + sig[i, 0]
        sim = ham[1] + sig[i, 1]
        wre = qre * sre - qim * sim
        wim = qre * sim + qim * sre
        wl = left_c(wre, wim)
        w2re, w2im = cmul(wl, right_c(wre, wim))
        w2r = right_c(w2re, w2im)
        w4re, w4im = cmul(left_c(w2re, w2im), w2r)
        tre, tim = cmul(wl, w2r)
        eye = (
            lax.broadcasted_iota(jnp.int32, (N, N), 0) == lax.broadcasted_iota(jnp.int32, (N, N), 1)
        ).astype(F32)
        are = eye + wre + w2re + tre
        aim = wim + w2im + tim
        bre, bim = cmul(left_c(are, aim), right_c(w4re, w4im))
        are = are + bre
        aim = aim + bim
        return qre * are - qim * aim, qre * aim + qim * are

    def swap(i):
        return pltpu.make_async_remote_copy(
            src_ref=gout.at[i], dst_ref=blocks.at[l], send_sem=swap_send, recv_sem=swap_recv,
            device_id=device(i, group, k), device_id_type=MESH,
        )

    half = pl.ds(pl.multiple_of(k * (N // 2), 8), N // 2)
    part = pl.ds(pl.multiple_of((k * XS + x) * PART, 8), PART)
    far = pl.ds(1, LAYERS - 1)

    def bond_copy(d):
        return pltpu.make_async_remote_copy(
            src_ref=bonds.at[0, part], dst_ref=bonds.at[LAYERS - d, part],
            send_sem=bond_send.at[0], recv_sem=bond_recv.at[0],
            device_id=device(ls[d], group, k), device_id_type=MESH,
        )

    def bond_share(rows, stage, target):
        return pltpu.make_async_remote_copy(
            src_ref=bonds.at[far, rows], dst_ref=bonds.at[far, rows],
            send_sem=bond_send.at[stage], recv_sem=bond_recv.at[stage],
            device_id=target, device_id_type=MESH,
        )

    bond_parts = [bonds.at[far, pl.ds(0, rows)] for rows in (PART, (XS - 1) * PART, N // 2)]

    def bond_wait(stage, semaphores):
        pltpu.make_async_copy(bond_parts[stage], bond_parts[stage], semaphores.at[stage]).wait()

    def keep(where, i, block):
        where[i, 0], where[i, 1] = block

    loads[0].wait()
    loads[1].wait()
    bonds[0] = coup[...] * pat[...].astype(F32)
    loads[2].wait()
    loads[3].wait()
    keep(gout, ls[2], inverse(ls[2]))
    pl.semaphore_wait(barrier, LAYERS + XS + 3)
    tell(z_sem, z_near)
    for d in (2, 1, 3):
        bond_copy(d).start()
    swap(ls[2]).start()

    loads[4].wait()
    loads[5].wait()
    one, two = inverse(ls[1]), inverse(ls[3])
    keep(gout, ls[1], one)
    keep(gout, ls[3], two)
    swap(ls[1]).start()
    swap(ls[3]).start()
    loads[6].wait()
    keep(blocks, l, inverse(l))
    bond_wait(0, bond_recv)
    for target in x_line:
        bond_share(part, 1, target).start()
    pl.semaphore_wait(z_sem, 4)
    tell(x_sem, x_line)
    pl.semaphore_wait(x_sem, XS - 1)
    tell(y_sem, y_line)
    bond_wait(1, bond_recv)
    bond_share(half, 2, other_core[0]).start()

    three = blocks.at[pl.ds(0, LAYERS - 1)]
    pltpu.make_async_copy(three, three, swap_recv).wait()
    bond_wait(2, bond_recv)
    pl.semaphore_wait(y_sem, LAYERS - 1)
    tell(core_sem, other_core)

    g = [(blocks[i, 0], blocks[i, 1]) for i in range(LAYERS)]

    def ends(i, first, second):
        re, im = g[i]
        stacked = split(jnp.concatenate([re, im], axis=0))
        head = dot(lhs3([stacked]), right_plain([first]))
        tail = dot(lhs3([second]), right_plain([split(re), split(im)]))
        return left_c(head[:N], head[N:]), right_c(tail[:, :N], tail[:, N:])

    down_ends, up_ends = {}, {}
    for i in range(1, LAYERS):
        b = bonds[wrap(i - l + LAYERS, LAYERS)]
        bs, bts = split(b), split(b.T)
        down_ends[i] = ends(i, bs, bts)
        up_ends[i - 1] = ends(i - 1, bts, bs)

    def dress(i, ends, inner):
        sre, sim = cmul(left_c(*cmul(ends[0], right_c(*inner))), ends[1])
        return g[i][0] + sre, g[i][1] + sim

    down = {0: g[0]}
    up = {LAYERS - 1: g[LAYERS - 1]}
    for step in range(1, LAYERS):
        down[step] = dress(step, down_ends[step], down[step - 1])
        j = LAYERS - 1 - step
        up[j] = dress(j, up_ends[j], up[j + 1])
    for c in range(2):
        zero = jnp.zeros((N, N), F32)
        greens[0, c] = zero
        greens[LAYERS + 1, c] = zero
        for i in range(LAYERS):
            greens[i + 1, c] = down[i][c] + (up[i][c] - g[i][c])

    rows = lax.broadcasted_iota(jnp.int32, (N, N), 0)
    cols = lax.broadcasted_iota(jnp.int32, (N, N), 1)
    upper = rows < cols
    slot = group * LAYERS + l

    def exchange(part, t):
        layer = ls[t]

        def forward(to_group, to_mom):
            pltpu.make_async_remote_copy(
                src_ref=send.at[part, layer, to_group * MOMS + to_mom],
                dst_ref=recv.at[part, k, slot],
                send_sem=fwd_send.at[part], recv_sem=fwd_recv.at[part],
                device_id=device(layer, to_group, to_mom), device_id_type=MESH,
            ).start()

        plane(forward)
        if t:
            forward(group, k)
        else:
            pltpu.make_async_copy(
                send.at[part, layer, group * MOMS + k], recv.at[part, k, slot], fwd_recv.at[part]
            ).start()

    pl.semaphore_wait(core_sem, 1)
    for t in (2, 1, 3, 0):
        layer = ls[t]
        yre = greens[layer + 1, 0] + 0.5 * (greens[layer, 0] + greens[layer + 2, 0])
        yim = greens[layer + 1, 1] + 0.5 * (greens[layer, 1] + greens[layer + 2, 1])
        tre, tim = yre.T, yim.T
        pmat = jnp.where(upper, yre - tre, yim + tim)
        qmat = jnp.where(upper, yim - tim, yre + tre)
        for part, mat in enumerate((pmat, qmat)):
            for r in range(2):
                send[part, layer, :, r, :] = mat[r * PEERS : (r + 1) * PEERS]
        exchange(0, t)
    for t in (2, 1, 3, 0):
        exchange(1, t)

    loads[7].wait()
    loads[8].wait()
    dist = rows - cols
    own = jnp.zeros((N, N), F32)
    other = jnp.zeros((N, N), F32)
    for m in range(PHONONS):
        own = own + jnp.where(dist == shift[m], weight[m], 0.0)
        other = other + jnp.where(dist == -shift[m], weight[m], 0.0)
    other = 0.5 * other
    occupation = 1.0 / (1.0 + jnp.exp(8.0 * cols.astype(F32) / ENERGIES - 4.0))
    ret_w = jnp.concatenate(
        [jnp.concatenate([own, other], axis=1), jnp.concatenate([other, own], axis=1)], axis=0
    )
    fown, fother = own * occupation, other * occupation
    les_w = jnp.concatenate(
        [jnp.concatenate([fown, fother], axis=1), jnp.concatenate([fother, fown], axis=1)], axis=0
    )
    ret_l = lhs3([split(ret_w)])
    both_l = jnp.concatenate([ret_l, lhs3([split(les_w)])], axis=0)

    spot = group * MOMS + k

    def mix(part, left, mixed, back, kinds):
        arrived = recv.at[part]
        pltpu.make_async_copy(arrived, arrived, fwd_recv.at[part]).wait()
        pieces = [
            split(jnp.concatenate([recv[part, 0, :, r, :], recv[part, 1, :, r, :]], axis=0))
            for r in range(2)
        ]
        out = dot(left, right_plain(pieces))
        each = 2 * kinds
        for kind in range(kinds):
            for c in range(MOMS):
                top = (kind * MOMS + c) * N
                for r in range(2):
                    mixed[c, pl.ds(2 * kind + r, N, stride=each), :] = out[
                        top : top + N, r * N : (r + 1) * N
                    ]
        size = each * LAYERS

        def source(to_group, to_mom):
            return mixed.at[to_mom, pl.ds(pl.multiple_of(to_group * size, 8), size), :]

        def returning(to_group, to_mom):
            pltpu.make_async_remote_copy(
                src_ref=source(to_group, to_mom), dst_ref=back.at[spot],
                send_sem=ret_send.at[part], recv_sem=ret_recv.at[part],
                device_id=device(l, to_group, to_mom), device_id_type=MESH,
            ).start()

        plane(returning)
        pltpu.make_async_copy(source(group, k), back.at[spot], ret_recv.at[part]).start()

    mix(0, both_l, mixed_p, back_p, 2)
    mix(1, ret_l, mixed_q, back_q, 1)

    for part, back in enumerate((back_p, back_q)):
        whole = back.at[pl.ds(0, PEERS)]
        pltpu.make_async_copy(whole, whole, ret_recv.at[part]).wait()
        sent = back.at[pl.ds(0, PEERS - 1)]
        pltpu.make_async_copy(sent, sent, ret_send.at[part]).wait()
        for i in range(LAYERS):
            gone = send.at[part, i] if i else send.at[part, 0, pl.ds(0, PEERS - 1)]
            pltpu.make_async_copy(gone, gone, fwd_send.at[part]).wait()
    pltpu.make_async_copy(three, three, swap_send).wait()
    for stage in range(3):
        bond_wait(stage, bond_send)


def unpack_kernel(back_p, back_q, ret, les):
    e = pl.program_id(0)
    rows = lax.broadcasted_iota(jnp.int32, (N, N), 0)
    cols = lax.broadcasted_iota(jnp.int32, (N, N), 1)
    upper = rows < cols

    def whole(back, each, r):
        return jnp.concatenate(
            [back[pl.ds(each * e + r + h, PEERS, stride=LAYERS * each), :] for h in range(2)],
            axis=0,
        )

    pmat, lmat, qmat = whole(back_p, 4, 0), whole(back_p, 4, 2), whole(back_q, 2, 0)
    pt, qt, lt = pmat.T, qmat.T, lmat.T
    off = rows != cols
    zero = jnp.zeros((N, N), F32)
    ret[0, 0, 0, 0] = 0.5 * jnp.where(upper, pmat + qt, qmat - jnp.where(off, pt, zero))
    ret[0, 0, 0, 1] = 0.5 * jnp.where(upper, pt + qmat, pmat - jnp.where(off, qt, zero))
    les[0, 0, 0, 0] = jnp.where(upper, lmat, jnp.where(off, -lt, zero))
    les[0, 0, 0, 1] = jnp.where(upper, lt, lmat)


def shards(hamiltonian, sigma_prev, coupling, coupling_pattern, phonon_shift, phonon_weight):
    dma = pltpu.SemaphoreType.DMA
    back_p, back_q = pl.pallas_call(
        main_kernel,
        out_shape=(
            pltpu.VMEM((PEERS + 1, 16, N), F32),
            pltpu.VMEM((PEERS + 1, 8, N), F32),
        ),
        in_specs=[pl.BlockSpec(memory_space=pl.ANY)] * 6,
        out_specs=(pl.BlockSpec(memory_space=pltpu.VMEM),) * 2,
        scratch_shapes=[
            pltpu.VMEM((2, N, N), F32),
            pltpu.VMEM((4, 2, N, N), F32),
            pltpu.VMEM((N, N), F32),
            pltpu.VMEM((N, N), jnp.int32),
            pltpu.SMEM((PHONONS,), jnp.int32),
            pltpu.SMEM((PHONONS,), F32),
            pltpu.VMEM((LAYERS, 2, N, N), F32),
            pltpu.VMEM((LAYERS, 2, N, N), F32),
            pltpu.VMEM((LAYERS, N, N), F32),
            pltpu.VMEM((LAYERS + 2, 2, N, N), F32),
            pltpu.VMEM((2, LAYERS, PEERS, 2, N), F32),
            pltpu.VMEM((2, MOMS, ENERGIES, 2, N), F32),
            pltpu.VMEM((MOMS, 4 * ENERGIES + 8, N), F32),
            pltpu.VMEM((MOMS, 2 * ENERGIES + 8, N), F32),
        ]
        + [dma] * 2
        + [dma((3,))] * 2
        + [dma((2,))] * 4
        + [dma((9,))]
        + [pltpu.SemaphoreType.REGULAR] * 4,
        compiler_params=pltpu.CompilerParams(collective_id=0, has_side_effects=True),
        name="selfenergy",
    )(
        hamiltonian[0, 0], sigma_prev[0, 0], coupling[0], coupling_pattern,
        phonon_shift, phonon_weight,
    )
    shape = jax.ShapeDtypeStruct((1, 1, 4, 2, N, N), F32)
    out_spec = pl.BlockSpec((1, 1, 1, 2, N, N), lambda e: (0, 0, e, 0, 0, 0))
    return pl.pallas_call(
        unpack_kernel,
        grid=(4,),
        out_shape=(shape, shape),
        in_specs=[
            pl.BlockSpec(memory_space=pltpu.VMEM),
            pl.BlockSpec(memory_space=pltpu.VMEM),
        ],
        out_specs=(out_spec, out_spec),
        name="unpack",
    )(*(
        pltpu.with_memory_space_constraint(back, pltpu.VMEM)
        for back in (back_p.reshape((PEERS + 1) * 16, N), back_q.reshape((PEERS + 1) * 8, N))
    ))


def solution(mesh):
    in_specs = (
        P("mom", "len", None, None, None),
        P("mom", "len", "energy", None, None, None),
        P("len", None, None),
        P(),
        P(),
        P(),
    )
    out_specs = (
        P("mom", "len", "energy", None, None, None),
        P("mom", "len", "energy", None, None, None),
    )
    return jax.shard_map(shards, mesh=mesh, in_specs=in_specs, out_specs=out_specs, check_vma=False)
```

```python
import functools

import jax
import jax.numpy as jnp
from jax import lax
from jax.experimental import pallas as pl
from jax.experimental.pallas import tpu as pltpu
from jax.sharding import PartitionSpec as P

N = 128
LAYERS = 4
ENERGIES = 128
GROUPS = 32
ZS, XS = 8, 4
MOMS = 2
PEERS = GROUPS * MOMS
PHONONS = 4
PART = N // (MOMS * XS)
ORDER = [(dx, dk) for dx in (2, 1, 3, 0) for dk in (1, 0)]
F32 = jnp.float32
BF16 = jnp.bfloat16
MESH = pl.DeviceIdType.MESH


def wrap(value, size):
    return jnp.where(value >= size, value - size, value)


def device(layer, group, mom):
    return (layer, group, mom)


def split(value):
    high = value.astype(BF16)
    return high, (value - high.astype(F32)).astype(BF16)


def lhs3(parts, axis=1):
    high = jnp.concatenate([p[0] for p in parts], axis=axis)
    low = jnp.concatenate([p[1] for p in parts], axis=axis)
    return jnp.concatenate([high, high, low], axis=1)


def dot(left, right):
    return jnp.dot(left, right, preferred_element_type=F32)


def left_c(re, im):
    return lhs3([split(re), split(im)])


def right_c(re, im):
    rh, rl = split(re)
    ih, il = split(im)
    high = jnp.concatenate(
        [jnp.concatenate([rh, ih], axis=1), jnp.concatenate([-ih, rh], axis=1)], axis=0
    )
    low = jnp.concatenate(
        [jnp.concatenate([rl, il], axis=1), jnp.concatenate([-il, rl], axis=1)], axis=0
    )
    return jnp.concatenate([high, low, high], axis=0)


def cmul(left, right):
    both = dot(left, right)
    return both[:, :N], both[:, N:]


def right_plain(parts):
    high = jnp.concatenate([p[0] for p in parts], axis=1)
    low = jnp.concatenate([p[1] for p in parts], axis=1)
    return jnp.concatenate([high, low, high], axis=0)


def main_kernel(
    ham_in, sig_in, coup_in, pat_in, shift_in, weight_in, back_p, back_q,
    ham, sig, coup, pat, shift, weight,
    gout, blocks, bonds, greens, send, recv, mixed_p, mixed_q,
    swap_send, swap_recv, bond_send, bond_recv,
    fwd_send, fwd_recv, ret_send, ret_recv, in_sems,
    z_sem, z_sem2, y_sem, turn_sem,
):
    l = lax.axis_index("len")
    group = lax.axis_index("energy")
    k = lax.axis_index("mom")
    z = group // XS
    x = group - z * XS
    ls = [wrap(l + i, LAYERS) for i in range(LAYERS)]
    xs = [wrap(x + i, XS) for i in range(XS)]
    ks = [k, 1 - k]

    def plane(body):
        def line(base, skip=0):
            for dx, dk in ORDER[: XS * MOMS - skip]:
                body(base + xs[dx], ks[dk])

        line(wrap(z + ZS // 2, ZS) * XS)

        def step(i, carry):
            ahead = wrap(z + ZS // 2 - i, ZS) * XS
            behind = wrap(z + ZS // 2 + i, ZS) * XS
            for dx, dk in ORDER:
                body(ahead + xs[dx], ks[dk])
                body(behind + xs[dx], ks[dk])
            return carry

        lax.fori_loop(1, ZS // 2, step, 0)
        line(z * XS, skip=1)

    def tell(semaphore, targets):
        for target in targets:
            pl.semaphore_signal(semaphore, inc=1, device_id=target, device_id_type=MESH)

    x_line = [device(l, z * XS + xs[i], k) for i in range(1, XS)]
    x_other = [device(l, z * XS + xs[i], 1 - k) for i in range(1, XS)]
    z_near = [device(l, wrap(z + i, ZS) * XS + x, k) for i in (1, 2, ZS - 2, ZS - 1)]
    y_line = [device(ls[i], group, k) for i in range(1, LAYERS)]
    other_core = [device(l, group, 1 - k)]
    barrier = pltpu.get_barrier_semaphore()
    tell(barrier, y_line + x_line + x_other + z_near + other_core)

    loads = [
        pltpu.make_async_copy(coup_in, coup, in_sems.at[0]),
        pltpu.make_async_copy(pat_in, pat, in_sems.at[1]),
        pltpu.make_async_copy(ham_in, ham, in_sems.at[2]),
        pltpu.make_async_copy(sig_in.at[ls[2]], sig.at[ls[2]], in_sems.at[3]),
        pltpu.make_async_copy(sig_in.at[ls[1]], sig.at[ls[1]], in_sems.at[4]),
        pltpu.make_async_copy(sig_in.at[ls[3]], sig.at[ls[3]], in_sems.at[5]),
        pltpu.make_async_copy(sig_in.at[l], sig.at[l], in_sems.at[6]),
        pltpu.make_async_copy(shift_in, shift, in_sems.at[7]),
        pltpu.make_async_copy(weight_in, weight, in_sems.at[8]),
    ]
    for load in loads:
        load.start()

    def inverse(i):
        e = (group * LAYERS + i).astype(F32)
        zre = 5.0 + 2.0 * e / ENERGIES
        mag = zre * zre + 1.0
        qre = jnp.full((1, 1), zre / mag, F32)
        qim = jnp.full((1, 1), -1.0 / mag, F32)
        sre = ham[0] + sig[i, 0]
        sim = ham[1] + sig[i, 1]
        wre = qre * sre - qim * sim
        wim = qre * sim + qim * sre
        wl = left_c(wre, wim)
        w2re, w2im = cmul(wl, right_c(wre, wim))
        w2r = right_c(w2re, w2im)
        w4re, w4im = cmul(left_c(w2re, w2im), w2r)
        tre, tim = cmul(wl, w2r)
        eye = (
            lax.broadcasted_iota(jnp.int32, (N, N), 0) == lax.broadcasted_iota(jnp.int32, (N, N), 1)
        ).astype(F32)
        are = eye + wre + w2re + tre
        aim = wim + w2im + tim
        bre, bim = cmul(left_c(are, aim), right_c(w4re, w4im))
        are = are + bre
        aim = aim + bim
        return qre * are - qim * aim, qre * aim + qim * are

    def swap(i):
        return pltpu.make_async_remote_copy(
            src_ref=gout.at[i], dst_ref=blocks.at[l], send_sem=swap_send, recv_sem=swap_recv,
            device_id=device(i, group, k), device_id_type=MESH,
        )

    half = pl.ds(pl.multiple_of(k * (N // 2), 8), N // 2)
    part = pl.ds(pl.multiple_of((k * XS + x) * PART, 8), PART)
    far = pl.ds(1, LAYERS - 1)

    def bond_copy(d):
        return pltpu.make_async_remote_copy(
            src_ref=bonds.at[0, part], dst_ref=bonds.at[LAYERS - d, part],
            send_sem=bond_send.at[0], recv_sem=bond_recv.at[0],
            device_id=device(ls[d], group, k), device_id_type=MESH,
        )

    def bond_share(rows, stage, target):
        return pltpu.make_async_remote_copy(
            src_ref=bonds.at[far, rows], dst_ref=bonds.at[far, rows],
            send_sem=bond_send.at[stage], recv_sem=bond_recv.at[stage],
            device_id=target, device_id_type=MESH,
        )

    bond_parts = [bonds.at[far, pl.ds(0, rows)] for rows in (PART, (XS - 1) * PART, N // 2)]

    def bond_wait(stage, semaphores):
        pltpu.make_async_copy(bond_parts[stage], bond_parts[stage], semaphores.at[stage]).wait()

    def keep(where, i, block):
        where[i, 0], where[i, 1] = block

    loads[0].wait()
    loads[1].wait()
    bonds[0] = coup[...] * pat[...].astype(F32)
    loads[2].wait()
    loads[3].wait()
    keep(gout, ls[2], inverse(ls[2]))
    pl.semaphore_wait(barrier, LAYERS + 2 * XS + 2)
    tell(z_sem, z_near)
    for d in (2, 1, 3):
        bond_copy(d).start()

    @pl.when(k == 0)
    def _():
        swap(ls[2]).start()

    loads[4].wait()
    loads[5].wait()
    one, two = inverse(ls[1]), inverse(ls[3])
    keep(gout, ls[1], one)
    keep(gout, ls[3], two)

    @pl.when(k == 0)
    def _():
        swap(ls[1]).start()
        swap(ls[3]).start()

    pl.semaphore_wait(z_sem, 4)
    tell(z_sem2, z_near)
    loads[6].wait()
    keep(blocks, l, inverse(l))

    three = blocks.at[pl.ds(0, LAYERS - 1)]

    @pl.when(k == 0)
    def _():
        tell(turn_sem, other_core)

    bond_wait(0, bond_recv)
    for target in x_line:
        bond_share(part, 1, target).start()

    @pl.when(k == 1)
    def _():
        pl.semaphore_wait(turn_sem, 1)
        for d in (2, 1, 3):
            swap(ls[d]).start()

    pl.semaphore_wait(z_sem2, 4)
    tell(y_sem, y_line)
    bond_wait(1, bond_recv)
    bond_share(half, 2, other_core[0]).start()

    pltpu.make_async_copy(three, three, swap_recv).wait()
    bond_wait(2, bond_recv)

    g = [(blocks[i, 0], blocks[i, 1]) for i in range(LAYERS)]

    def ends(i, first, second):
        re, im = g[i]
        stacked = split(jnp.concatenate([re, im], axis=0))
        head = dot(lhs3([stacked]), right_plain([first]))
        tail = dot(lhs3([second]), right_plain([split(re), split(im)]))
        return left_c(head[:N], head[N:]), right_c(tail[:, :N], tail[:, N:])

    down_ends, up_ends = {}, {}
    for i in range(1, LAYERS):
        b = bonds[wrap(i - l + LAYERS, LAYERS)]
        bs, bts = split(b), split(b.T)
        down_ends[i] = ends(i, bs, bts)
        up_ends[i - 1] = ends(i - 1, bts, bs)

    def dress(i, ends, inner):
        sre, sim = cmul(left_c(*cmul(ends[0], right_c(*inner))), ends[1])
        return g[i][0] + sre, g[i][1] + sim

    down = {0: g[0]}
    up = {LAYERS - 1: g[LAYERS - 1]}
    for step in range(1, LAYERS):
        down[step] = dress(step, down_ends[step], down[step - 1])
        j = LAYERS - 1 - step
        up[j] = dress(j, up_ends[j], up[j + 1])
    for c in range(2):
        zero = jnp.zeros((N, N), F32)
        greens[0, c] = zero
        greens[LAYERS + 1, c] = zero
        for i in range(LAYERS):
            greens[i + 1, c] = down[i][c] + (up[i][c] - g[i][c])

    rows = lax.broadcasted_iota(jnp.int32, (N, N), 0)
    cols = lax.broadcasted_iota(jnp.int32, (N, N), 1)
    upper = rows < cols
    slot = group * LAYERS + l

    def exchange(part, t):
        layer = ls[t]

        def forward(to_group, to_mom):
            pltpu.make_async_remote_copy(
                src_ref=send.at[part, layer, to_group * MOMS + to_mom],
                dst_ref=recv.at[part, k, slot],
                send_sem=fwd_send.at[part], recv_sem=fwd_recv.at[part],
                device_id=device(layer, to_group, to_mom), device_id_type=MESH,
            ).start()

        plane(forward)
        if t:
            forward(group, k)
        else:
            pltpu.make_async_copy(
                send.at[part, layer, group * MOMS + k], recv.at[part, k, slot], fwd_recv.at[part]
            ).start()

    pl.semaphore_wait(y_sem, LAYERS - 1)
    for t in (2, 1, 3, 0):
        layer = ls[t]
        yre = greens[layer + 1, 0] + 0.5 * (greens[layer, 0] + greens[layer + 2, 0])
        yim = greens[layer + 1, 1] + 0.5 * (greens[layer, 1] + greens[layer + 2, 1])
        tre, tim = yre.T, yim.T
        pmat = jnp.where(upper, yre - tre, yim + tim)
        qmat = jnp.where(upper, yim - tim, yre + tre)
        for part, mat in enumerate((pmat, qmat)):
            for r in range(2):
                send[part, layer, :, r, :] = mat[r * PEERS : (r + 1) * PEERS]
        exchange(0, t)
    for t in (2, 1, 3, 0):
        exchange(1, t)

    loads[7].wait()
    loads[8].wait()
    dist = rows - cols
    own = jnp.zeros((N, N), F32)
    other = jnp.zeros((N, N), F32)
    for m in range(PHONONS):
        own = own + jnp.where(dist == shift[m], weight[m], 0.0)
        other = other + jnp.where(dist == -shift[m], weight[m], 0.0)
    other = 0.5 * other
    occupation = 1.0 / (1.0 + jnp.exp(8.0 * cols.astype(F32) / ENERGIES - 4.0))
    ret_w = jnp.concatenate(
        [jnp.concatenate([own, other], axis=1), jnp.concatenate([other, own], axis=1)], axis=0
    )
    fown, fother = own * occupation, other * occupation
    les_w = jnp.concatenate(
        [jnp.concatenate([fown, fother], axis=1), jnp.concatenate([fother, fown], axis=1)], axis=0
    )
    ret_l = lhs3([split(ret_w)])
    both_l = jnp.concatenate([ret_l, lhs3([split(les_w)])], axis=0)

    spot = group * MOMS + k

    def mix(part, left, mixed, back, kinds):
        arrived = recv.at[part]
        pltpu.make_async_copy(arrived, arrived, fwd_recv.at[part]).wait()
        pieces = [
            split(jnp.concatenate([recv[part, 0, :, r, :], recv[part, 1, :, r, :]], axis=0))
            for r in range(2)
        ]
        out = dot(left, right_plain(pieces))
        each = 2 * kinds
        for kind in range(kinds):
            for c in range(MOMS):
                top = (kind * MOMS + c) * N
                for r in range(2):
                    mixed[c, pl.ds(2 * kind + r, N, stride=each), :] = out[
                        top : top + N, r * N : (r + 1) * N
                    ]
        size = each * LAYERS

        def source(to_group, to_mom):
            return mixed.at[to_mom, pl.ds(pl.multiple_of(to_group * size, 8), size), :]

        def returning(to_group, to_mom):
            pltpu.make_async_remote_copy(
                src_ref=source(to_group, to_mom), dst_ref=back.at[spot],
                send_sem=ret_send.at[part], recv_sem=ret_recv.at[part],
                device_id=device(l, to_group, to_mom), device_id_type=MESH,
            ).start()

        plane(returning)
        pltpu.make_async_copy(source(group, k), back.at[spot], ret_recv.at[part]).start()

    mix(0, both_l, mixed_p, back_p, 2)
    mix(1, ret_l, mixed_q, back_q, 1)

    for part, back in enumerate((back_p, back_q)):
        whole = back.at[pl.ds(0, PEERS)]
        pltpu.make_async_copy(whole, whole, ret_recv.at[part]).wait()
        sent = back.at[pl.ds(0, PEERS - 1)]
        pltpu.make_async_copy(sent, sent, ret_send.at[part]).wait()
        for i in range(LAYERS):
            gone = send.at[part, i] if i else send.at[part, 0, pl.ds(0, PEERS - 1)]
            pltpu.make_async_copy(gone, gone, fwd_send.at[part]).wait()
    pltpu.make_async_copy(three, three, swap_send).wait()
    for stage in range(3):
        bond_wait(stage, bond_send)


def unpack_kernel(back_p, back_q, ret, les):
    e = pl.program_id(0)
    rows = lax.broadcasted_iota(jnp.int32, (N, N), 0)
    cols = lax.broadcasted_iota(jnp.int32, (N, N), 1)
    upper = rows < cols

    def whole(back, each, r):
        return jnp.concatenate(
            [back[pl.ds(each * e + r + h, PEERS, stride=LAYERS * each), :] for h in range(2)],
            axis=0,
        )

    pmat, lmat, qmat = whole(back_p, 4, 0), whole(back_p, 4, 2), whole(back_q, 2, 0)
    pt, qt, lt = pmat.T, qmat.T, lmat.T
    off = rows != cols
    zero = jnp.zeros((N, N), F32)
    ret[0, 0, 0, 0] = 0.5 * jnp.where(upper, pmat + qt, qmat - jnp.where(off, pt, zero))
    ret[0, 0, 0, 1] = 0.5 * jnp.where(upper, pt + qmat, pmat - jnp.where(off, qt, zero))
    les[0, 0, 0, 0] = jnp.where(upper, lmat, jnp.where(off, -lt, zero))
    les[0, 0, 0, 1] = jnp.where(upper, lt, lmat)


def shards(hamiltonian, sigma_prev, coupling, coupling_pattern, phonon_shift, phonon_weight):
    dma = pltpu.SemaphoreType.DMA
    back_p, back_q = pl.pallas_call(
        main_kernel,
        out_shape=(
            pltpu.VMEM((PEERS + 1, 16, N), F32),
            pltpu.VMEM((PEERS + 1, 8, N), F32),
        ),
        in_specs=[pl.BlockSpec(memory_space=pl.ANY)] * 6,
        out_specs=(pl.BlockSpec(memory_space=pltpu.VMEM),) * 2,
        scratch_shapes=[
            pltpu.VMEM((2, N, N), F32),
            pltpu.VMEM((4, 2, N, N), F32),
            pltpu.VMEM((N, N), F32),
            pltpu.VMEM((N, N), jnp.int32),
            pltpu.SMEM((PHONONS,), jnp.int32),
            pltpu.SMEM((PHONONS,), F32),
            pltpu.VMEM((LAYERS, 2, N, N), F32),
            pltpu.VMEM((LAYERS, 2, N, N), F32),
            pltpu.VMEM((LAYERS, N, N), F32),
            pltpu.VMEM((LAYERS + 2, 2, N, N), F32),
            pltpu.VMEM((2, LAYERS, PEERS, 2, N), F32),
            pltpu.VMEM((2, MOMS, ENERGIES, 2, N), F32),
            pltpu.VMEM((MOMS, 4 * ENERGIES + 8, N), F32),
            pltpu.VMEM((MOMS, 2 * ENERGIES + 8, N), F32),
        ]
        + [dma] * 2
        + [dma((3,))] * 2
        + [dma((2,))] * 4
        + [dma((9,))]
        + [pltpu.SemaphoreType.REGULAR] * 4,
        compiler_params=pltpu.CompilerParams(collective_id=0, has_side_effects=True),
        name="selfenergy",
    )(
        hamiltonian[0, 0], sigma_prev[0, 0], coupling[0], coupling_pattern,
        phonon_shift, phonon_weight,
    )
    shape = jax.ShapeDtypeStruct((1, 1, 4, 2, N, N), F32)
    out_spec = pl.BlockSpec((1, 1, 1, 2, N, N), lambda e: (0, 0, e, 0, 0, 0))
    return pl.pallas_call(
        unpack_kernel,
        grid=(4,),
        out_shape=(shape, shape),
        in_specs=[
            pl.BlockSpec(memory_space=pltpu.VMEM),
            pl.BlockSpec(memory_space=pltpu.VMEM),
        ],
        out_specs=(out_spec, out_spec),
        name="unpack",
    )(*(
        pltpu.with_memory_space_constraint(back, pltpu.VMEM)
        for back in (back_p.reshape((PEERS + 1) * 16, N), back_q.reshape((PEERS + 1) * 8, N))
    ))


def solution(mesh):
    in_specs = (
        P("mom", "len", None, None, None),
        P("mom", "len", "energy", None, None, None),
        P("len", None, None),
        P(),
        P(),
        P(),
    )
    out_specs = (
        P("mom", "len", "energy", None, None, None),
        P("mom", "len", "energy", None, None, None),
    )
    return jax.shard_map(shards, mesh=mesh, in_specs=in_specs, out_specs=out_specs, check_vma=False)
```

```python
import functools

import jax
import jax.numpy as jnp
from jax import lax
from jax.experimental import pallas as pl
from jax.experimental.pallas import tpu as pltpu
from jax.sharding import PartitionSpec as P

N = 128
LAYERS = 4
ENERGIES = 128
GROUPS = 32
ZS, XS = 8, 4
MOMS = 2
PEERS = GROUPS * MOMS
PHONONS = 4
PART = N // (MOMS * XS)
ORDER = [(dx, dk) for dx in (2, 1, 3, 0) for dk in (1, 0)]
F32 = jnp.float32
BF16 = jnp.bfloat16
MESH = pl.DeviceIdType.MESH


def wrap(value, size):
    return jnp.where(value >= size, value - size, value)


def device(layer, group, mom):
    return (layer, group, mom)


def split(value):
    high = value.astype(BF16)
    return high, (value - high.astype(F32)).astype(BF16)


def lhs3(parts, axis=1):
    high = jnp.concatenate([p[0] for p in parts], axis=axis)
    low = jnp.concatenate([p[1] for p in parts], axis=axis)
    return jnp.concatenate([high, high, low], axis=1)


def dot(left, right):
    return jnp.dot(left, right, preferred_element_type=F32)


def left_c(re, im):
    return lhs3([split(re), split(im)])


def right_c(re, im):
    rh, rl = split(re)
    ih, il = split(im)
    high = jnp.concatenate(
        [jnp.concatenate([rh, ih], axis=1), jnp.concatenate([-ih, rh], axis=1)], axis=0
    )
    low = jnp.concatenate(
        [jnp.concatenate([rl, il], axis=1), jnp.concatenate([-il, rl], axis=1)], axis=0
    )
    return jnp.concatenate([high, low, high], axis=0)


def cmul(left, right):
    both = dot(left, right)
    return both[:, :N], both[:, N:]


def right_plain(parts):
    high = jnp.concatenate([p[0] for p in parts], axis=1)
    low = jnp.concatenate([p[1] for p in parts], axis=1)
    return jnp.concatenate([high, low, high], axis=0)


def gather(back, each, i, first):
    return jnp.concatenate(
        [back[pl.ds(each * i + first + h, PEERS, stride=LAYERS * each), :] for h in range(2)],
        axis=0,
    )


def main_kernel(
    ham_in, sig_in, coup_in, pat_in, shift_in, weight_in, lesser, base, back_q,
    ham, sig, coup, pat, shift, weight,
    gout, blocks, bonds, greens, send, recv, mixed_p, mixed_q, back_p,
    swap_send, swap_recv, bond_send, bond_recv,
    fwd_send, fwd_recv, ret_send, ret_recv, in_sems,
    z_sem, z_sem2, y_sem, turn_sem,
):
    l = lax.axis_index("len")
    group = lax.axis_index("energy")
    k = lax.axis_index("mom")
    z = group // XS
    x = group - z * XS
    ls = [wrap(l + i, LAYERS) for i in range(LAYERS)]
    xs = [wrap(x + i, XS) for i in range(XS)]
    ks = [k, 1 - k]

    def plane(body):
        def line(base, skip=0):
            for dx, dk in ORDER[: XS * MOMS - skip]:
                body(base + xs[dx], ks[dk])

        line(wrap(z + ZS // 2, ZS) * XS)

        def step(i, carry):
            ahead = wrap(z + ZS // 2 - i, ZS) * XS
            behind = wrap(z + ZS // 2 + i, ZS) * XS
            for dx, dk in ORDER:
                body(ahead + xs[dx], ks[dk])
                body(behind + xs[dx], ks[dk])
            return carry

        lax.fori_loop(1, ZS // 2, step, 0)
        line(z * XS, skip=1)

    def tell(semaphore, targets):
        for target in targets:
            pl.semaphore_signal(semaphore, inc=1, device_id=target, device_id_type=MESH)

    x_line = [device(l, z * XS + xs[i], k) for i in range(1, XS)]
    x_other = [device(l, z * XS + xs[i], 1 - k) for i in range(1, XS)]
    z_near = [device(l, wrap(z + i, ZS) * XS + x, k) for i in (1, 2, ZS - 2, ZS - 1)]
    y_line = [device(ls[i], group, k) for i in range(1, LAYERS)]
    other_core = [device(l, group, 1 - k)]
    barrier = pltpu.get_barrier_semaphore()
    tell(barrier, y_line + x_line + x_other + z_near + other_core)

    loads = [
        pltpu.make_async_copy(coup_in, coup, in_sems.at[0]),
        pltpu.make_async_copy(pat_in, pat, in_sems.at[1]),
        pltpu.make_async_copy(ham_in, ham, in_sems.at[2]),
        pltpu.make_async_copy(sig_in.at[ls[2]], sig.at[ls[2]], in_sems.at[3]),
        pltpu.make_async_copy(sig_in.at[ls[1]], sig.at[ls[1]], in_sems.at[4]),
        pltpu.make_async_copy(sig_in.at[ls[3]], sig.at[ls[3]], in_sems.at[5]),
        pltpu.make_async_copy(sig_in.at[l], sig.at[l], in_sems.at[6]),
        pltpu.make_async_copy(shift_in, shift, in_sems.at[7]),
        pltpu.make_async_copy(weight_in, weight, in_sems.at[8]),
    ]
    for load in loads:
        load.start()

    def inverse(i):
        e = (group * LAYERS + i).astype(F32)
        zre = 5.0 + 2.0 * e / ENERGIES
        mag = zre * zre + 1.0
        qre = jnp.full((1, 1), zre / mag, F32)
        qim = jnp.full((1, 1), -1.0 / mag, F32)
        sre = ham[0] + sig[i, 0]
        sim = ham[1] + sig[i, 1]
        wre = qre * sre - qim * sim
        wim = qre * sim + qim * sre
        wl = left_c(wre, wim)
        w2re, w2im = cmul(wl, right_c(wre, wim))
        w2r = right_c(w2re, w2im)
        w4re, w4im = cmul(left_c(w2re, w2im), w2r)
        tre, tim = cmul(wl, w2r)
        eye = (
            lax.broadcasted_iota(jnp.int32, (N, N), 0) == lax.broadcasted_iota(jnp.int32, (N, N), 1)
        ).astype(F32)
        are = eye + wre + w2re + tre
        aim = wim + w2im + tim
        bre, bim = cmul(left_c(are, aim), right_c(w4re, w4im))
        are = are + bre
        aim = aim + bim
        return qre * are - qim * aim, qre * aim + qim * are

    def swap(i):
        return pltpu.make_async_remote_copy(
            src_ref=gout.at[i], dst_ref=blocks.at[l], send_sem=swap_send, recv_sem=swap_recv,
            device_id=device(i, group, k), device_id_type=MESH,
        )

    half = pl.ds(pl.multiple_of(k * (N // 2), 8), N // 2)
    part = pl.ds(pl.multiple_of((k * XS + x) * PART, 8), PART)
    far = pl.ds(1, LAYERS - 1)

    def bond_copy(d):
        return pltpu.make_async_remote_copy(
            src_ref=bonds.at[0, part], dst_ref=bonds.at[LAYERS - d, part],
            send_sem=bond_send.at[0], recv_sem=bond_recv.at[0],
            device_id=device(ls[d], group, k), device_id_type=MESH,
        )

    def bond_share(rows, stage, target):
        return pltpu.make_async_remote_copy(
            src_ref=bonds.at[far, rows], dst_ref=bonds.at[far, rows],
            send_sem=bond_send.at[stage], recv_sem=bond_recv.at[stage],
            device_id=target, device_id_type=MESH,
        )

    bond_parts = [bonds.at[far, pl.ds(0, rows)] for rows in (PART, (XS - 1) * PART, N // 2)]

    def bond_wait(stage, semaphores):
        pltpu.make_async_copy(bond_parts[stage], bond_parts[stage], semaphores.at[stage]).wait()

    def keep(where, i, block):
        where[i, 0], where[i, 1] = block

    loads[0].wait()
    loads[1].wait()
    bonds[0] = coup[...] * pat[...].astype(F32)
    loads[2].wait()
    loads[3].wait()
    keep(gout, ls[2], inverse(ls[2]))
    pl.semaphore_wait(barrier, LAYERS + 2 * XS + 2)
    tell(z_sem, z_near)
    for d in (2, 1, 3):
        bond_copy(d).start()

    @pl.when(k == 0)
    def _():
        swap(ls[2]).start()

    loads[4].wait()
    loads[5].wait()
    one, two = inverse(ls[1]), inverse(ls[3])
    keep(gout, ls[1], one)
    keep(gout, ls[3], two)

    @pl.when(k == 0)
    def _():
        swap(ls[1]).start()
        swap(ls[3]).start()

    pl.semaphore_wait(z_sem, 4)
    tell(z_sem2, z_near)
    loads[6].wait()
    keep(blocks, l, inverse(l))

    three = blocks.at[pl.ds(0, LAYERS - 1)]

    @pl.when(k == 0)
    def _():
        tell(turn_sem, other_core)

    bond_wait(0, bond_recv)
    for target in x_line:
        bond_share(part, 1, target).start()

    @pl.when(k == 1)
    def _():
        pl.semaphore_wait(turn_sem, 1)
        for d in (2, 1, 3):
            swap(ls[d]).start()

    pl.semaphore_wait(z_sem2, 4)
    tell(y_sem, y_line)
    bond_wait(1, bond_recv)
    bond_share(half, 2, other_core[0]).start()

    pltpu.make_async_copy(three, three, swap_recv).wait()
    bond_wait(2, bond_recv)

    g = [(blocks[i, 0], blocks[i, 1]) for i in range(LAYERS)]

    def ends(i, first, second):
        re, im = g[i]
        stacked = split(jnp.concatenate([re, im], axis=0))
        head = dot(lhs3([stacked]), right_plain([first]))
        tail = dot(lhs3([second]), right_plain([split(re), split(im)]))
        return left_c(head[:N], head[N:]), right_c(tail[:, :N], tail[:, N:])

    down_ends, up_ends = {}, {}
    for i in range(1, LAYERS):
        b = bonds[wrap(i - l + LAYERS, LAYERS)]
        bs, bts = split(b), split(b.T)
        down_ends[i] = ends(i, bs, bts)
        up_ends[i - 1] = ends(i - 1, bts, bs)

    def dress(i, ends, inner):
        sre, sim = cmul(left_c(*cmul(ends[0], right_c(*inner))), ends[1])
        return g[i][0] + sre, g[i][1] + sim

    down = {0: g[0]}
    up = {LAYERS - 1: g[LAYERS - 1]}
    for step in range(1, LAYERS):
        down[step] = dress(step, down_ends[step], down[step - 1])
        j = LAYERS - 1 - step
        up[j] = dress(j, up_ends[j], up[j + 1])
    for c in range(2):
        zero = jnp.zeros((N, N), F32)
        greens[0, c] = zero
        greens[LAYERS + 1, c] = zero
        for i in range(LAYERS):
            greens[i + 1, c] = down[i][c] + (up[i][c] - g[i][c])

    rows = lax.broadcasted_iota(jnp.int32, (N, N), 0)
    cols = lax.broadcasted_iota(jnp.int32, (N, N), 1)
    upper = rows < cols
    slot = group * LAYERS + l

    def exchange(part, t):
        layer = ls[t]

        def forward(to_group, to_mom):
            pltpu.make_async_remote_copy(
                src_ref=send.at[part, layer, to_group * MOMS + to_mom],
                dst_ref=recv.at[part, k, slot],
                send_sem=fwd_send.at[part], recv_sem=fwd_recv.at[part],
                device_id=device(layer, to_group, to_mom), device_id_type=MESH,
            ).start()

        plane(forward)
        if t:
            forward(group, k)
        else:
            pltpu.make_async_copy(
                send.at[part, layer, group * MOMS + k], recv.at[part, k, slot], fwd_recv.at[part]
            ).start()

    pl.semaphore_wait(y_sem, LAYERS - 1)
    for t in (2, 1, 3, 0):
        layer = ls[t]
        yre = greens[layer + 1, 0] + 0.5 * (greens[layer, 0] + greens[layer + 2, 0])
        yim = greens[layer + 1, 1] + 0.5 * (greens[layer, 1] + greens[layer + 2, 1])
        tre, tim = yre.T, yim.T
        pmat = jnp.where(upper, yre - tre, yim + tim)
        qmat = jnp.where(upper, yim - tim, yre + tre)
        for part, mat in enumerate((pmat, qmat)):
            for r in range(2):
                send[part, layer, :, r, :] = mat[r * PEERS : (r + 1) * PEERS]
        exchange(0, t)
    for t in (2, 1, 3, 0):
        exchange(1, t)

    loads[7].wait()
    loads[8].wait()
    dist = rows - cols
    own = jnp.zeros((N, N), F32)
    other = jnp.zeros((N, N), F32)
    for m in range(PHONONS):
        own = own + jnp.where(dist == shift[m], weight[m], 0.0)
        other = other + jnp.where(dist == -shift[m], weight[m], 0.0)
    other = 0.5 * other
    occupation = 1.0 / (1.0 + jnp.exp(8.0 * cols.astype(F32) / ENERGIES - 4.0))
    ret_w = jnp.concatenate(
        [jnp.concatenate([own, other], axis=1), jnp.concatenate([other, own], axis=1)], axis=0
    )
    fown, fother = own * occupation, other * occupation
    les_w = jnp.concatenate(
        [jnp.concatenate([fown, fother], axis=1), jnp.concatenate([fother, fown], axis=1)], axis=0
    )
    ret_l = lhs3([split(ret_w)])
    both_l = jnp.concatenate([ret_l, lhs3([split(les_w)])], axis=0)

    def mix(part, left, mixed, back, kinds):
        arrived = recv.at[part]
        pltpu.make_async_copy(arrived, arrived, fwd_recv.at[part]).wait()
        pieces = [
            split(jnp.concatenate([recv[part, 0, :, r, :], recv[part, 1, :, r, :]], axis=0))
            for r in range(2)
        ]
        out = dot(left, right_plain(pieces))
        each = 2 * kinds
        for kind in range(kinds):
            for c in range(MOMS):
                top = (kind * MOMS + c) * N
                for r in range(2):
                    mixed[c, pl.ds(2 * kind + r, N, stride=each), :] = out[
                        top : top + N, r * N : (r + 1) * N
                    ]
        size = each * LAYERS
        spot = pl.ds(pl.multiple_of((group * MOMS + k) * size, 8), size)

        def source(to_group, to_mom):
            return mixed.at[to_mom, pl.ds(pl.multiple_of(to_group * size, 8), size), :]

        def returning(to_group, to_mom):
            pltpu.make_async_remote_copy(
                src_ref=source(to_group, to_mom), dst_ref=back.at[spot],
                send_sem=ret_send.at[part], recv_sem=ret_recv.at[part],
                device_id=device(l, to_group, to_mom), device_id_type=MESH,
            ).start()

        plane(returning)
        pltpu.make_async_copy(source(group, k), back.at[spot], ret_recv.at[part]).start()

    mix(0, both_l, mixed_p, back_p, 2)
    mix(1, ret_l, mixed_q, back_q, 1)

    def arrive(part, back, size):
        whole = back.at[pl.ds(0, PEERS * size)]
        pltpu.make_async_copy(whole, whole, ret_recv.at[part]).wait()

    arrive(0, back_p, 16)
    off = rows != cols
    zero = jnp.zeros((N, N), F32)
    for i in range(LAYERS):
        pmat, lmat = gather(back_p, 4, i, 0), gather(back_p, 4, i, 2)
        pt, lt = pmat.T, lmat.T
        lesser[i, 0] = jnp.where(upper, lmat, jnp.where(off, -lt, zero))
        lesser[i, 1] = jnp.where(upper, lt, lmat)
        base[i, 0] = 0.5 * jnp.where(upper, pmat, jnp.where(off, -pt, zero))
        base[i, 1] = 0.5 * jnp.where(upper, pt, pmat)
    arrive(1, back_q, 8)

    for part, (back, size) in enumerate(((back_p, 16), (back_q, 8))):
        sent = back.at[pl.ds(0, (PEERS - 1) * size)]
        pltpu.make_async_copy(sent, sent, ret_send.at[part]).wait()
        for i in range(LAYERS):
            gone = send.at[part, i] if i else send.at[part, 0, pl.ds(0, PEERS - 1)]
            pltpu.make_async_copy(gone, gone, fwd_send.at[part]).wait()
    pltpu.make_async_copy(three, three, swap_send).wait()
    for stage in range(3):
        bond_wait(stage, bond_send)


def unpack_kernel(lesser, base, back_q, ret, les, out, sems):
    lesser_copy = pltpu.make_async_copy(lesser, les.at[0, 0], sems.at[LAYERS])
    lesser_copy.start()
    rows = lax.broadcasted_iota(jnp.int32, (N, N), 0)
    cols = lax.broadcasted_iota(jnp.int32, (N, N), 1)
    upper = rows < cols
    off = rows != cols
    zero = jnp.zeros((N, N), F32)
    copies = [
        pltpu.make_async_copy(out.at[i], ret.at[0, 0, i], sems.at[i]) for i in range(LAYERS)
    ]
    for i in range(LAYERS):
        qmat = gather(back_q, 2, i, 0)
        qt = qmat.T
        out[i, 0] = base[i, 0] + 0.5 * jnp.where(upper, qt, qmat)
        out[i, 1] = base[i, 1] + 0.5 * jnp.where(upper, qmat, jnp.where(off, -qt, zero))
        copies[i].start()
    for copy in copies:
        copy.wait()
    lesser_copy.wait()


def shards(hamiltonian, sigma_prev, coupling, coupling_pattern, phonon_shift, phonon_weight):
    dma = pltpu.SemaphoreType.DMA
    found = pl.pallas_call(
        main_kernel,
        out_shape=(
            pltpu.VMEM((LAYERS, 2, N, N), F32),
            pltpu.VMEM((LAYERS, 2, N, N), F32),
            pltpu.VMEM(((PEERS + 1) * 8, N), F32),
        ),
        in_specs=[pl.BlockSpec(memory_space=pl.ANY)] * 6,
        out_specs=(pl.BlockSpec(memory_space=pltpu.VMEM),) * 3,
        scratch_shapes=[
            pltpu.VMEM((2, N, N), F32),
            pltpu.VMEM((4, 2, N, N), F32),
            pltpu.VMEM((N, N), F32),
            pltpu.VMEM((N, N), jnp.int32),
            pltpu.SMEM((PHONONS,), jnp.int32),
            pltpu.SMEM((PHONONS,), F32),
            pltpu.VMEM((LAYERS, 2, N, N), F32),
            pltpu.VMEM((LAYERS, 2, N, N), F32),
            pltpu.VMEM((LAYERS, N, N), F32),
            pltpu.VMEM((LAYERS + 2, 2, N, N), F32),
            pltpu.VMEM((2, LAYERS, PEERS, 2, N), F32),
            pltpu.VMEM((2, MOMS, ENERGIES, 2, N), F32),
            pltpu.VMEM((MOMS, 4 * ENERGIES + 8, N), F32),
            pltpu.VMEM((MOMS, 2 * ENERGIES + 8, N), F32),
            pltpu.VMEM(((PEERS + 1) * 16, N), F32),
        ]
        + [dma] * 2
        + [dma((3,))] * 2
        + [dma((2,))] * 4
        + [dma((9,))]
        + [pltpu.SemaphoreType.REGULAR] * 4,
        compiler_params=pltpu.CompilerParams(collective_id=0, has_side_effects=True),
        name="selfenergy",
    )(
        hamiltonian[0, 0], sigma_prev[0, 0], coupling[0], coupling_pattern,
        phonon_shift, phonon_weight,
    )
    shape = jax.ShapeDtypeStruct((1, 1, 4, 2, N, N), F32)
    return pl.pallas_call(
        unpack_kernel,
        out_shape=(shape, shape),
        in_specs=[pl.BlockSpec(memory_space=pltpu.VMEM)] * 3,
        out_specs=(pl.BlockSpec(memory_space=pl.ANY),) * 2,
        scratch_shapes=[pltpu.VMEM((LAYERS, 2, N, N), F32), dma((LAYERS + 1,))],
        name="unpack",
    )(*(pltpu.with_memory_space_constraint(value, pltpu.VMEM) for value in found))


def solution(mesh):
    in_specs = (
        P("mom", "len", None, None, None),
        P("mom", "len", "energy", None, None, None),
        P("len", None, None),
        P(),
        P(),
        P(),
    )
    out_specs = (
        P("mom", "len", "energy", None, None, None),
        P("mom", "len", "energy", None, None, None),
    )
    return jax.shard_map(shards, mesh=mesh, in_specs=in_specs, out_specs=out_specs, check_vma=False)
```

```python
import functools

import jax
import jax.numpy as jnp
from jax import lax
from jax.experimental import pallas as pl
from jax.experimental.pallas import tpu as pltpu
from jax.sharding import PartitionSpec as P

N = 128
LAYERS = 4
ENERGIES = 128
GROUPS = 32
ZS, XS = 8, 4
MOMS = 2
PEERS = GROUPS * MOMS
PHONONS = 4
PART = N // (MOMS * XS)
ORDER = [(dx, dk) for dx in (2, 1, 3, 0) for dk in (1, 0)]
F32 = jnp.float32
BF16 = jnp.bfloat16
MESH = pl.DeviceIdType.MESH


def wrap(value, size):
    return jnp.where(value >= size, value - size, value)


def device(layer, group, mom):
    return (layer, group, mom)


def split(value):
    high = value.astype(BF16)
    return high, (value - high.astype(F32)).astype(BF16)


def lhs3(parts, axis=1):
    high = jnp.concatenate([p[0] for p in parts], axis=axis)
    low = jnp.concatenate([p[1] for p in parts], axis=axis)
    return jnp.concatenate([high, high, low], axis=1)


def dot(left, right):
    return jnp.dot(left, right, preferred_element_type=F32)


def left_c(re, im):
    return lhs3([split(re), split(im)])


def right_c(re, im):
    rh, rl = split(re)
    ih, il = split(im)
    high = jnp.concatenate(
        [jnp.concatenate([rh, ih], axis=1), jnp.concatenate([-ih, rh], axis=1)], axis=0
    )
    low = jnp.concatenate(
        [jnp.concatenate([rl, il], axis=1), jnp.concatenate([-il, rl], axis=1)], axis=0
    )
    return jnp.concatenate([high, low, high], axis=0)


def cmul(left, right):
    both = dot(left, right)
    return both[:, :N], both[:, N:]


def right_plain(parts):
    high = jnp.concatenate([p[0] for p in parts], axis=1)
    low = jnp.concatenate([p[1] for p in parts], axis=1)
    return jnp.concatenate([high, low, high], axis=0)


def gather(back, each, i, first):
    return jnp.concatenate(
        [back[pl.ds(each * i + first + h, PEERS, stride=LAYERS * each), :] for h in range(2)],
        axis=0,
    )


def main_kernel(
    ham_in, sig_in, coup_in, pat_in, shift_in, weight_in, lesser, base, back_q,
    ham, sig, coup, pat, shift, weight,
    gout, blocks, bonds, greens, send, recv, mixed_p, mixed_q, back_p,
    swap_send, swap_recv, bond_send, bond_recv,
    fwd_send, fwd_recv, ret_send, ret_recv, in_sems,
    z_sem, z_sem2, y_sem, turn_sem,
):
    l = lax.axis_index("len")
    group = lax.axis_index("energy")
    k = lax.axis_index("mom")
    z = group // XS
    x = group - z * XS
    ls = [wrap(l + i, LAYERS) for i in range(LAYERS)]
    xs = [wrap(x + i, XS) for i in range(XS)]
    ks = [k, 1 - k]

    def plane(body):
        def line(base, skip=0):
            for dx, dk in ORDER[: XS * MOMS - skip]:
                body(base + xs[dx], ks[dk])

        line(wrap(z + ZS // 2, ZS) * XS)

        def step(i, carry):
            ahead = wrap(z + ZS // 2 - i, ZS) * XS
            behind = wrap(z + ZS // 2 + i, ZS) * XS
            for dx, dk in ORDER:
                body(ahead + xs[dx], ks[dk])
                body(behind + xs[dx], ks[dk])
            return carry

        lax.fori_loop(1, ZS // 2, step, 0)
        line(z * XS, skip=1)

    def tell(semaphore, targets):
        for target in targets:
            pl.semaphore_signal(semaphore, inc=1, device_id=target, device_id_type=MESH)

    x_line = [device(l, z * XS + xs[i], k) for i in range(1, XS)]
    x_other = [device(l, z * XS + xs[i], 1 - k) for i in range(1, XS)]
    z_near = [device(l, wrap(z + i, ZS) * XS + x, k) for i in (1, 2, ZS - 2, ZS - 1)]
    y_line = [device(ls[i], group, k) for i in range(1, LAYERS)]
    other_core = [device(l, group, 1 - k)]
    barrier = pltpu.get_barrier_semaphore()
    tell(barrier, y_line + x_line + x_other + z_near + other_core)

    loads = [
        pltpu.make_async_copy(coup_in, coup, in_sems.at[0]),
        pltpu.make_async_copy(pat_in, pat, in_sems.at[1]),
        pltpu.make_async_copy(ham_in, ham, in_sems.at[2]),
        pltpu.make_async_copy(sig_in.at[ls[2]], sig.at[ls[2]], in_sems.at[3]),
        pltpu.make_async_copy(sig_in.at[ls[1]], sig.at[ls[1]], in_sems.at[4]),
        pltpu.make_async_copy(sig_in.at[ls[3]], sig.at[ls[3]], in_sems.at[5]),
        pltpu.make_async_copy(sig_in.at[l], sig.at[l], in_sems.at[6]),
        pltpu.make_async_copy(shift_in, shift, in_sems.at[7]),
        pltpu.make_async_copy(weight_in, weight, in_sems.at[8]),
    ]
    for load in loads:
        load.start()

    def inverse(i):
        e = (group * LAYERS + i).astype(F32)
        zre = 5.0 + 2.0 * e / ENERGIES
        mag = zre * zre + 1.0
        qre = jnp.full((1, 1), zre / mag, F32)
        qim = jnp.full((1, 1), -1.0 / mag, F32)
        sre = ham[0] + sig[i, 0]
        sim = ham[1] + sig[i, 1]
        wre = qre * sre - qim * sim
        wim = qre * sim + qim * sre
        wl = left_c(wre, wim)
        w2re, w2im = cmul(wl, right_c(wre, wim))
        w2r = right_c(w2re, w2im)
        w4re, w4im = cmul(left_c(w2re, w2im), w2r)
        tre, tim = cmul(wl, w2r)
        eye = (
            lax.broadcasted_iota(jnp.int32, (N, N), 0) == lax.broadcasted_iota(jnp.int32, (N, N), 1)
        ).astype(F32)
        are = eye + wre + w2re + tre
        aim = wim + w2im + tim
        bre, bim = cmul(left_c(are, aim), right_c(w4re, w4im))
        are = are + bre
        aim = aim + bim
        return qre * are - qim * aim, qre * aim + qim * are

    def swap(i):
        return pltpu.make_async_remote_copy(
            src_ref=gout.at[i], dst_ref=blocks.at[l], send_sem=swap_send, recv_sem=swap_recv,
            device_id=device(i, group, k), device_id_type=MESH,
        )

    half = pl.ds(pl.multiple_of(k * (N // 2), 8), N // 2)
    part = pl.ds(pl.multiple_of((k * XS + x) * PART, 8), PART)
    far = pl.ds(1, LAYERS - 1)

    def bond_copy(d):
        return pltpu.make_async_remote_copy(
            src_ref=bonds.at[0, part], dst_ref=bonds.at[LAYERS - d, part],
            send_sem=bond_send.at[0], recv_sem=bond_recv.at[0],
            device_id=device(ls[d], group, k), device_id_type=MESH,
        )

    def bond_share(rows, stage, target):
        return pltpu.make_async_remote_copy(
            src_ref=bonds.at[far, rows], dst_ref=bonds.at[far, rows],
            send_sem=bond_send.at[stage], recv_sem=bond_recv.at[stage],
            device_id=target, device_id_type=MESH,
        )

    bond_parts = [bonds.at[far, pl.ds(0, rows)] for rows in (PART, (XS - 1) * PART, N // 2)]

    def bond_wait(stage, semaphores):
        pltpu.make_async_copy(bond_parts[stage], bond_parts[stage], semaphores.at[stage]).wait()

    def keep(where, i, block):
        where[i, 0], where[i, 1] = block

    loads[0].wait()
    loads[1].wait()
    bonds[0] = coup[...] * pat[...].astype(F32)
    loads[2].wait()
    loads[3].wait()
    keep(gout, ls[2], inverse(ls[2]))
    pl.semaphore_wait(barrier, LAYERS + 2 * XS + 2)
    tell(z_sem, z_near)
    for d in (2, 1, 3):
        bond_copy(d).start()

    @pl.when(k == 0)
    def _():
        swap(ls[2]).start()

    loads[4].wait()
    loads[5].wait()
    one, two = inverse(ls[1]), inverse(ls[3])
    keep(gout, ls[1], one)
    keep(gout, ls[3], two)

    @pl.when(k == 0)
    def _():
        swap(ls[1]).start()
        swap(ls[3]).start()

    pl.semaphore_wait(z_sem, 4)
    tell(z_sem2, z_near)
    loads[6].wait()
    keep(blocks, l, inverse(l))

    three = blocks.at[pl.ds(0, LAYERS - 1)]

    @pl.when(k == 0)
    def _():
        pltpu.make_async_copy(three, three, swap_send).wait()
        tell(turn_sem, other_core)

    bond_wait(0, bond_recv)
    for target in x_line:
        bond_share(part, 1, target).start()

    @pl.when(k == 1)
    def _():
        pl.semaphore_wait(turn_sem, 1)
        for d in (2, 1, 3):
            swap(ls[d]).start()

    pl.semaphore_wait(z_sem2, 4)
    tell(y_sem, y_line)
    bond_wait(1, bond_recv)
    bond_share(half, 2, other_core[0]).start()

    pltpu.make_async_copy(three, three, swap_recv).wait()
    bond_wait(2, bond_recv)

    g = [(blocks[i, 0], blocks[i, 1]) for i in range(LAYERS)]

    def ends(i, first, second):
        re, im = g[i]
        stacked = split(jnp.concatenate([re, im], axis=0))
        head = dot(lhs3([stacked]), right_plain([first]))
        tail = dot(lhs3([second]), right_plain([split(re), split(im)]))
        return left_c(head[:N], head[N:]), right_c(tail[:, :N], tail[:, N:])

    down_ends, up_ends = {}, {}
    for i in range(1, LAYERS):
        b = bonds[wrap(i - l + LAYERS, LAYERS)]
        bs, bts = split(b), split(b.T)
        down_ends[i] = ends(i, bs, bts)
        up_ends[i - 1] = ends(i - 1, bts, bs)

    def dress(i, ends, inner):
        sre, sim = cmul(left_c(*cmul(ends[0], right_c(*inner))), ends[1])
        return g[i][0] + sre, g[i][1] + sim

    down = {0: g[0]}
    up = {LAYERS - 1: g[LAYERS - 1]}
    for step in range(1, LAYERS):
        down[step] = dress(step, down_ends[step], down[step - 1])
        j = LAYERS - 1 - step
        up[j] = dress(j, up_ends[j], up[j + 1])
    for c in range(2):
        zero = jnp.zeros((N, N), F32)
        greens[0, c] = zero
        greens[LAYERS + 1, c] = zero
        for i in range(LAYERS):
            greens[i + 1, c] = down[i][c] + (up[i][c] - g[i][c])

    rows = lax.broadcasted_iota(jnp.int32, (N, N), 0)
    cols = lax.broadcasted_iota(jnp.int32, (N, N), 1)
    upper = rows < cols
    slot = group * LAYERS + l

    def exchange(part, t):
        layer = ls[t]

        def forward(to_group, to_mom):
            pltpu.make_async_remote_copy(
                src_ref=send.at[part, layer, to_group * MOMS + to_mom],
                dst_ref=recv.at[part, k, slot],
                send_sem=fwd_send.at[part], recv_sem=fwd_recv.at[part],
                device_id=device(layer, to_group, to_mom), device_id_type=MESH,
            ).start()

        plane(forward)
        if t:
            forward(group, k)
        else:
            pltpu.make_async_copy(
                send.at[part, layer, group * MOMS + k], recv.at[part, k, slot], fwd_recv.at[part]
            ).start()

    pl.semaphore_wait(y_sem, LAYERS - 1)
    for t in (2, 1, 3, 0):
        layer = ls[t]
        yre = greens[layer + 1, 0] + 0.5 * (greens[layer, 0] + greens[layer + 2, 0])
        yim = greens[layer + 1, 1] + 0.5 * (greens[layer, 1] + greens[layer + 2, 1])
        tre, tim = yre.T, yim.T
        pmat = jnp.where(upper, yre - tre, yim + tim)
        qmat = jnp.where(upper, yim - tim, yre + tre)
        for part, mat in enumerate((pmat, qmat)):
            for r in range(2):
                send[part, layer, :, r, :] = mat[r * PEERS : (r + 1) * PEERS]
        exchange(0, t)
    for t in (2, 1, 3, 0):
        exchange(1, t)

    loads[7].wait()
    loads[8].wait()
    dist = rows - cols
    own = jnp.zeros((N, N), F32)
    other = jnp.zeros((N, N), F32)
    for m in range(PHONONS):
        own = own + jnp.where(dist == shift[m], weight[m], 0.0)
        other = other + jnp.where(dist == -shift[m], weight[m], 0.0)
    other = 0.5 * other
    occupation = 1.0 / (1.0 + jnp.exp(8.0 * cols.astype(F32) / ENERGIES - 4.0))
    ret_w = jnp.concatenate(
        [jnp.concatenate([own, other], axis=1), jnp.concatenate([other, own], axis=1)], axis=0
    )
    fown, fother = own * occupation, other * occupation
    les_w = jnp.concatenate(
        [jnp.concatenate([fown, fother], axis=1), jnp.concatenate([fother, fown], axis=1)], axis=0
    )
    ret_l = lhs3([split(ret_w)])
    both_l = jnp.concatenate([ret_l, lhs3([split(les_w)])], axis=0)

    def mix(part, left, mixed, back, kinds):
        arrived = recv.at[part]
        pltpu.make_async_copy(arrived, arrived, fwd_recv.at[part]).wait()
        pieces = [
            split(jnp.concatenate([recv[part, 0, :, r, :], recv[part, 1, :, r, :]], axis=0))
            for r in range(2)
        ]
        out = dot(left, right_plain(pieces))
        each = 2 * kinds
        for kind in range(kinds):
            for c in range(MOMS):
                top = (kind * MOMS + c) * N
                for r in range(2):
                    mixed[c, pl.ds(2 * kind + r, N, stride=each), :] = out[
                        top : top + N, r * N : (r + 1) * N
                    ]
        size = each * LAYERS
        spot = pl.ds(pl.multiple_of((group * MOMS + k) * size, 8), size)

        def source(to_group, to_mom):
            return mixed.at[to_mom, pl.ds(pl.multiple_of(to_group * size, 8), size), :]

        def returning(to_group, to_mom):
            pltpu.make_async_remote_copy(
                src_ref=source(to_group, to_mom), dst_ref=back.at[spot],
                send_sem=ret_send.at[part], recv_sem=ret_recv.at[part],
                device_id=device(l, to_group, to_mom), device_id_type=MESH,
            ).start()

        plane(returning)
        pltpu.make_async_copy(source(group, k), back.at[spot], ret_recv.at[part]).start()

    mix(0, both_l, mixed_p, back_p, 2)
    mix(1, ret_l, mixed_q, back_q, 1)

    def arrive(part, back, size):
        whole = back.at[pl.ds(0, PEERS * size)]
        pltpu.make_async_copy(whole, whole, ret_recv.at[part]).wait()

    arrive(0, back_p, 16)
    off = rows != cols
    zero = jnp.zeros((N, N), F32)
    for i in range(LAYERS):
        pmat, lmat = gather(back_p, 4, i, 0), gather(back_p, 4, i, 2)
        pt, lt = pmat.T, lmat.T
        lesser[i, 0] = jnp.where(upper, lmat, jnp.where(off, -lt, zero))
        lesser[i, 1] = jnp.where(upper, lt, lmat)
        base[i, 0] = 0.5 * jnp.where(upper, pmat, jnp.where(off, -pt, zero))
        base[i, 1] = 0.5 * jnp.where(upper, pt, pmat)
    arrive(1, back_q, 8)

    for part, (back, size) in enumerate(((back_p, 16), (back_q, 8))):
        sent = back.at[pl.ds(0, (PEERS - 1) * size)]
        pltpu.make_async_copy(sent, sent, ret_send.at[part]).wait()
        for i in range(LAYERS):
            gone = send.at[part, i] if i else send.at[part, 0, pl.ds(0, PEERS - 1)]
            pltpu.make_async_copy(gone, gone, fwd_send.at[part]).wait()
    @pl.when(k == 1)
    def _():
        pltpu.make_async_copy(three, three, swap_send).wait()

    for stage in range(3):
        bond_wait(stage, bond_send)


def unpack_kernel(lesser, base, back_q, ret, les, out, sems):
    lesser_copy = pltpu.make_async_copy(lesser, les.at[0, 0], sems.at[LAYERS])
    lesser_copy.start()
    rows = lax.broadcasted_iota(jnp.int32, (N, N), 0)
    cols = lax.broadcasted_iota(jnp.int32, (N, N), 1)
    upper = rows < cols
    off = rows != cols
    zero = jnp.zeros((N, N), F32)
    copies = [
        pltpu.make_async_copy(out.at[i], ret.at[0, 0, i], sems.at[i]) for i in range(LAYERS)
    ]
    for i in range(LAYERS):
        qmat = gather(back_q, 2, i, 0)
        qt = qmat.T
        out[i, 0] = base[i, 0] + 0.5 * jnp.where(upper, qt, qmat)
        out[i, 1] = base[i, 1] + 0.5 * jnp.where(upper, qmat, jnp.where(off, -qt, zero))
        copies[i].start()
    for copy in copies:
        copy.wait()
    lesser_copy.wait()


def shards(hamiltonian, sigma_prev, coupling, coupling_pattern, phonon_shift, phonon_weight):
    dma = pltpu.SemaphoreType.DMA
    found = pl.pallas_call(
        main_kernel,
        out_shape=(
            pltpu.VMEM((LAYERS, 2, N, N), F32),
            pltpu.VMEM((LAYERS, 2, N, N), F32),
            pltpu.VMEM(((PEERS + 1) * 8, N), F32),
        ),
        in_specs=[pl.BlockSpec(memory_space=pl.ANY)] * 6,
        out_specs=(pl.BlockSpec(memory_space=pltpu.VMEM),) * 3,
        scratch_shapes=[
            pltpu.VMEM((2, N, N), F32),
            pltpu.VMEM((4, 2, N, N), F32),
            pltpu.VMEM((N, N), F32),
            pltpu.VMEM((N, N), jnp.int32),
            pltpu.SMEM((PHONONS,), jnp.int32),
            pltpu.SMEM((PHONONS,), F32),
            pltpu.VMEM((LAYERS, 2, N, N), F32),
            pltpu.VMEM((LAYERS, 2, N, N), F32),
            pltpu.VMEM((LAYERS, N, N), F32),
            pltpu.VMEM((LAYERS + 2, 2, N, N), F32),
            pltpu.VMEM((2, LAYERS, PEERS, 2, N), F32),
            pltpu.VMEM((2, MOMS, ENERGIES, 2, N), F32),
            pltpu.VMEM((MOMS, 4 * ENERGIES + 8, N), F32),
            pltpu.VMEM((MOMS, 2 * ENERGIES + 8, N), F32),
            pltpu.VMEM(((PEERS + 1) * 16, N), F32),
        ]
        + [dma] * 2
        + [dma((3,))] * 2
        + [dma((2,))] * 4
        + [dma((9,))]
        + [pltpu.SemaphoreType.REGULAR] * 4,
        compiler_params=pltpu.CompilerParams(collective_id=0, has_side_effects=True),
        name="selfenergy",
    )(
        hamiltonian[0, 0], sigma_prev[0, 0], coupling[0], coupling_pattern,
        phonon_shift, phonon_weight,
    )
    shape = jax.ShapeDtypeStruct((1, 1, 4, 2, N, N), F32)
    return pl.pallas_call(
        unpack_kernel,
        out_shape=(shape, shape),
        in_specs=[pl.BlockSpec(memory_space=pltpu.VMEM)] * 3,
        out_specs=(pl.BlockSpec(memory_space=pl.ANY),) * 2,
        scratch_shapes=[pltpu.VMEM((LAYERS, 2, N, N), F32), dma((LAYERS + 1,))],
        name="unpack",
    )(*(pltpu.with_memory_space_constraint(value, pltpu.VMEM) for value in found))


def solution(mesh):
    in_specs = (
        P("mom", "len", None, None, None),
        P("mom", "len", "energy", None, None, None),
        P("len", None, None),
        P(),
        P(),
        P(),
    )
    out_specs = (
        P("mom", "len", "energy", None, None, None),
        P("mom", "len", "energy", None, None, None),
    )
    return jax.shard_map(shards, mesh=mesh, in_specs=in_specs, out_specs=out_specs, check_vma=False)
```

```python
import functools

import jax
import jax.numpy as jnp
from jax import lax
from jax.experimental import pallas as pl
from jax.experimental.pallas import tpu as pltpu
from jax.sharding import PartitionSpec as P

N = 128
LAYERS = 4
ENERGIES = 128
GROUPS = 32
ZS, XS = 8, 4
MOMS = 2
PEERS = GROUPS * MOMS
PHONONS = 4
PART = N // (MOMS * XS)
ORDER = [(dx, dk) for dx in (2, 1, 3, 0) for dk in (1, 0)]
F32 = jnp.float32
BF16 = jnp.bfloat16
MESH = pl.DeviceIdType.MESH


def wrap(value, size):
    return jnp.where(value >= size, value - size, value)


def device(layer, group, mom):
    return (layer, group, mom)


def split(value):
    high = value.astype(BF16)
    return high, (value - high.astype(F32)).astype(BF16)


def lhs3(parts, axis=1):
    high = jnp.concatenate([p[0] for p in parts], axis=axis)
    low = jnp.concatenate([p[1] for p in parts], axis=axis)
    return jnp.concatenate([high, high, low], axis=1)


def dot(left, right):
    return jnp.dot(left, right, preferred_element_type=F32)


def left_c(re, im):
    return lhs3([split(re), split(im)])


def right_c(re, im):
    rh, rl = split(re)
    ih, il = split(im)
    high = jnp.concatenate(
        [jnp.concatenate([rh, ih], axis=1), jnp.concatenate([-ih, rh], axis=1)], axis=0
    )
    low = jnp.concatenate(
        [jnp.concatenate([rl, il], axis=1), jnp.concatenate([-il, rl], axis=1)], axis=0
    )
    return jnp.concatenate([high, low, high], axis=0)


def cmul(left, right):
    both = dot(left, right)
    return both[:, :N], both[:, N:]


def right_plain(parts):
    high = jnp.concatenate([p[0] for p in parts], axis=1)
    low = jnp.concatenate([p[1] for p in parts], axis=1)
    return jnp.concatenate([high, low, high], axis=0)


def gather(back, each, i, first):
    return jnp.concatenate(
        [back[pl.ds(each * i + first + h, PEERS, stride=LAYERS * each), :] for h in range(2)],
        axis=0,
    )


def main_kernel(
    ham_in, sig_in, coup_in, pat_in, shift_in, weight_in, lesser, base, back_q,
    ham, sig, coup, pat, shift, weight,
    gout, blocks, bonds, greens, send, recv, mixed_p, mixed_q, back_p,
    swap_send, swap_recv, bond_send, bond_recv,
    fwd_send, fwd_recv, ret_send, ret_recv, in_sems,
    z_sem, z_sem2, y_sem, turn_sem,
):
    l = lax.axis_index("len")
    group = lax.axis_index("energy")
    k = lax.axis_index("mom")
    z = group // XS
    x = group - z * XS
    ls = [wrap(l + i, LAYERS) for i in range(LAYERS)]
    xs = [wrap(x + i, XS) for i in range(XS)]
    ks = [k, 1 - k]

    def plane(body):
        def line(base, skip=0):
            for dx, dk in ORDER[: XS * MOMS - skip]:
                body(base + xs[dx], ks[dk])

        line(wrap(z + ZS // 2, ZS) * XS)

        def step(i, carry):
            ahead = wrap(z + ZS // 2 - i, ZS) * XS
            behind = wrap(z + ZS // 2 + i, ZS) * XS
            for dx, dk in ORDER:
                body(ahead + xs[dx], ks[dk])
                body(behind + xs[dx], ks[dk])
            return carry

        lax.fori_loop(1, ZS // 2, step, 0)
        line(z * XS, skip=1)

    def tell(semaphore, targets):
        for target in targets:
            pl.semaphore_signal(semaphore, inc=1, device_id=target, device_id_type=MESH)

    x_line = [device(l, z * XS + xs[i], k) for i in range(1, XS)]
    x_other = [device(l, z * XS + xs[i], 1 - k) for i in range(1, XS)]
    z_near = [device(l, wrap(z + i, ZS) * XS + x, k) for i in (1, 2, ZS - 2, ZS - 1)]
    y_line = [device(ls[i], group, k) for i in range(1, LAYERS)]
    other_core = [device(l, group, 1 - k)]
    barrier = pltpu.get_barrier_semaphore()
    tell(barrier, y_line + x_line + x_other + z_near + other_core)

    loads = [
        pltpu.make_async_copy(coup_in, coup, in_sems.at[0]),
        pltpu.make_async_copy(pat_in, pat, in_sems.at[1]),
        pltpu.make_async_copy(ham_in, ham, in_sems.at[2]),
        pltpu.make_async_copy(sig_in.at[ls[2]], sig.at[ls[2]], in_sems.at[3]),
        pltpu.make_async_copy(sig_in.at[ls[1]], sig.at[ls[1]], in_sems.at[4]),
        pltpu.make_async_copy(sig_in.at[ls[3]], sig.at[ls[3]], in_sems.at[5]),
        pltpu.make_async_copy(sig_in.at[l], sig.at[l], in_sems.at[6]),
        pltpu.make_async_copy(shift_in, shift, in_sems.at[7]),
        pltpu.make_async_copy(weight_in, weight, in_sems.at[8]),
    ]
    for load in loads:
        load.start()

    def inverse(i):
        e = (group * LAYERS + i).astype(F32)
        zre = 5.0 + 2.0 * e / ENERGIES
        mag = zre * zre + 1.0
        qre = jnp.full((1, 1), zre / mag, F32)
        qim = jnp.full((1, 1), -1.0 / mag, F32)
        sre = ham[0] + sig[i, 0]
        sim = ham[1] + sig[i, 1]
        wre = qre * sre - qim * sim
        wim = qre * sim + qim * sre
        wl = left_c(wre, wim)
        w2re, w2im = cmul(wl, right_c(wre, wim))
        w2r = right_c(w2re, w2im)
        w4re, w4im = cmul(left_c(w2re, w2im), w2r)
        tre, tim = cmul(wl, w2r)
        eye = (
            lax.broadcasted_iota(jnp.int32, (N, N), 0) == lax.broadcasted_iota(jnp.int32, (N, N), 1)
        ).astype(F32)
        are = eye + wre + w2re + tre
        aim = wim + w2im + tim
        bre, bim = cmul(left_c(are, aim), right_c(w4re, w4im))
        are = are + bre
        aim = aim + bim
        return qre * are - qim * aim, qre * aim + qim * are

    def swap(i):
        return pltpu.make_async_remote_copy(
            src_ref=gout.at[i], dst_ref=blocks.at[l], send_sem=swap_send, recv_sem=swap_recv,
            device_id=device(i, group, k), device_id_type=MESH,
        )

    half = pl.ds(pl.multiple_of(k * (N // 2), 8), N // 2)
    part = pl.ds(pl.multiple_of((k * XS + x) * PART, 8), PART)
    far = pl.ds(1, LAYERS - 1)

    def bond_copy(d):
        return pltpu.make_async_remote_copy(
            src_ref=bonds.at[0, part], dst_ref=bonds.at[LAYERS - d, part],
            send_sem=bond_send.at[0], recv_sem=bond_recv.at[0],
            device_id=device(ls[d], group, k), device_id_type=MESH,
        )

    def bond_share(rows, stage, target):
        return pltpu.make_async_remote_copy(
            src_ref=bonds.at[far, rows], dst_ref=bonds.at[far, rows],
            send_sem=bond_send.at[stage], recv_sem=bond_recv.at[stage],
            device_id=target, device_id_type=MESH,
        )

    bond_parts = [bonds.at[far, pl.ds(0, rows)] for rows in (PART, (XS - 1) * PART, N // 2)]

    def bond_wait(stage, semaphores):
        pltpu.make_async_copy(bond_parts[stage], bond_parts[stage], semaphores.at[stage]).wait()

    def keep(where, i, block):
        where[i, 0], where[i, 1] = block

    loads[0].wait()
    loads[1].wait()
    bonds[0] = coup[...] * pat[...].astype(F32)
    loads[2].wait()
    loads[3].wait()
    keep(gout, ls[2], inverse(ls[2]))
    pl.semaphore_wait(barrier, LAYERS + 2 * XS + 2)
    tell(z_sem, z_near)
    for d in (2, 1, 3):
        bond_copy(d).start()

    @pl.when(k == 0)
    def _():
        swap(ls[2]).start()

    loads[4].wait()
    loads[5].wait()
    one, two = inverse(ls[1]), inverse(ls[3])
    keep(gout, ls[1], one)
    keep(gout, ls[3], two)

    @pl.when(k == 0)
    def _():
        swap(ls[1]).start()
        swap(ls[3]).start()

    pl.semaphore_wait(z_sem, 4)
    tell(z_sem2, z_near)
    loads[6].wait()
    keep(blocks, l, inverse(l))

    three = blocks.at[pl.ds(0, LAYERS - 1)]

    bond_wait(0, bond_recv)
    for target in x_line:
        bond_share(part, 1, target).start()

    @pl.when(k == 0)
    def _():
        pltpu.make_async_copy(three, three, swap_send).wait()
        tell(turn_sem, other_core)

    @pl.when(k == 1)
    def _():
        pl.semaphore_wait(turn_sem, 1)
        for d in (2, 1, 3):
            swap(ls[d]).start()

    pl.semaphore_wait(z_sem2, 4)
    tell(y_sem, y_line)
    bond_wait(1, bond_recv)
    bond_share(half, 2, other_core[0]).start()

    pltpu.make_async_copy(three, three, swap_recv).wait()
    bond_wait(2, bond_recv)

    g = [(blocks[i, 0], blocks[i, 1]) for i in range(LAYERS)]

    def ends(i, first, second):
        re, im = g[i]
        stacked = split(jnp.concatenate([re, im], axis=0))
        head = dot(lhs3([stacked]), right_plain([first]))
        tail = dot(lhs3([second]), right_plain([split(re), split(im)]))
        return left_c(head[:N], head[N:]), right_c(tail[:, :N], tail[:, N:])

    down_ends, up_ends = {}, {}
    for i in range(1, LAYERS):
        b = bonds[wrap(i - l + LAYERS, LAYERS)]
        bs, bts = split(b), split(b.T)
        down_ends[i] = ends(i, bs, bts)
        up_ends[i - 1] = ends(i - 1, bts, bs)

    def dress(i, ends, inner):
        sre, sim = cmul(left_c(*cmul(ends[0], right_c(*inner))), ends[1])
        return g[i][0] + sre, g[i][1] + sim

    down = {0: g[0]}
    up = {LAYERS - 1: g[LAYERS - 1]}
    for step in range(1, LAYERS):
        down[step] = dress(step, down_ends[step], down[step - 1])
        j = LAYERS - 1 - step
        up[j] = dress(j, up_ends[j], up[j + 1])
    for c in range(2):
        zero = jnp.zeros((N, N), F32)
        greens[0, c] = zero
        greens[LAYERS + 1, c] = zero
        for i in range(LAYERS):
            greens[i + 1, c] = down[i][c] + (up[i][c] - g[i][c])

    rows = lax.broadcasted_iota(jnp.int32, (N, N), 0)
    cols = lax.broadcasted_iota(jnp.int32, (N, N), 1)
    upper = rows < cols
    slot = group * LAYERS + l

    def exchange(part, t):
        layer = ls[t]

        def forward(to_group, to_mom):
            pltpu.make_async_remote_copy(
                src_ref=send.at[part, layer, to_group * MOMS + to_mom],
                dst_ref=recv.at[part, k, slot],
                send_sem=fwd_send.at[part], recv_sem=fwd_recv.at[part],
                device_id=device(layer, to_group, to_mom), device_id_type=MESH,
            ).start()

        plane(forward)
        if t:
            forward(group, k)
        else:
            pltpu.make_async_copy(
                send.at[part, layer, group * MOMS + k], recv.at[part, k, slot], fwd_recv.at[part]
            ).start()

    pl.semaphore_wait(y_sem, LAYERS - 1)
    for t in (2, 1, 3, 0):
        layer = ls[t]
        yre = greens[layer + 1, 0] + 0.5 * (greens[layer, 0] + greens[layer + 2, 0])
        yim = greens[layer + 1, 1] + 0.5 * (greens[layer, 1] + greens[layer + 2, 1])
        tre, tim = yre.T, yim.T
        pmat = jnp.where(upper, yre - tre, yim + tim)
        qmat = jnp.where(upper, yim - tim, yre + tre)
        for part, mat in enumerate((pmat, qmat)):
            for r in range(2):
                send[part, layer, :, r, :] = mat[r * PEERS : (r + 1) * PEERS]
        exchange(0, t)
    for t in (2, 1, 3, 0):
        exchange(1, t)

    loads[7].wait()
    loads[8].wait()
    dist = rows - cols
    own = jnp.zeros((N, N), F32)
    other = jnp.zeros((N, N), F32)
    for m in range(PHONONS):
        own = own + jnp.where(dist == shift[m], weight[m], 0.0)
        other = other + jnp.where(dist == -shift[m], weight[m], 0.0)
    other = 0.5 * other
    occupation = 1.0 / (1.0 + jnp.exp(8.0 * cols.astype(F32) / ENERGIES - 4.0))
    ret_w = jnp.concatenate(
        [jnp.concatenate([own, other], axis=1), jnp.concatenate([other, own], axis=1)], axis=0
    )
    fown, fother = own * occupation, other * occupation
    les_w = jnp.concatenate(
        [jnp.concatenate([fown, fother], axis=1), jnp.concatenate([fother, fown], axis=1)], axis=0
    )
    ret_l = lhs3([split(ret_w)])
    both_l = jnp.concatenate([ret_l, lhs3([split(les_w)])], axis=0)

    def mix(part, left, mixed, back, kinds):
        arrived = recv.at[part]
        pltpu.make_async_copy(arrived, arrived, fwd_recv.at[part]).wait()
        pieces = [
            split(jnp.concatenate([recv[part, 0, :, r, :], recv[part, 1, :, r, :]], axis=0))
            for r in range(2)
        ]
        out = dot(left, right_plain(pieces))
        each = 2 * kinds
        for kind in range(kinds):
            for c in range(MOMS):
                top = (kind * MOMS + c) * N
                for r in range(2):
                    mixed[c, pl.ds(2 * kind + r, N, stride=each), :] = out[
                        top : top + N, r * N : (r + 1) * N
                    ]
        size = each * LAYERS
        spot = pl.ds(pl.multiple_of((group * MOMS + k) * size, 8), size)

        def source(to_group, to_mom):
            return mixed.at[to_mom, pl.ds(pl.multiple_of(to_group * size, 8), size), :]

        def returning(to_group, to_mom):
            pltpu.make_async_remote_copy(
                src_ref=source(to_group, to_mom), dst_ref=back.at[spot],
                send_sem=ret_send.at[part], recv_sem=ret_recv.at[part],
                device_id=device(l, to_group, to_mom), device_id_type=MESH,
            ).start()

        plane(returning)
        pltpu.make_async_copy(source(group, k), back.at[spot], ret_recv.at[part]).start()

    mix(0, both_l, mixed_p, back_p, 2)
    mix(1, ret_l, mixed_q, back_q, 1)

    def arrive(part, back, size):
        whole = back.at[pl.ds(0, PEERS * size)]
        pltpu.make_async_copy(whole, whole, ret_recv.at[part]).wait()

    arrive(0, back_p, 16)
    off = rows != cols
    zero = jnp.zeros((N, N), F32)
    for i in range(LAYERS):
        pmat, lmat = gather(back_p, 4, i, 0), gather(back_p, 4, i, 2)
        pt, lt = pmat.T, lmat.T
        lesser[i, 0] = jnp.where(upper, lmat, jnp.where(off, -lt, zero))
        lesser[i, 1] = jnp.where(upper, lt, lmat)
        base[i, 0] = 0.5 * jnp.where(upper, pmat, jnp.where(off, -pt, zero))
        base[i, 1] = 0.5 * jnp.where(upper, pt, pmat)
    arrive(1, back_q, 8)

    for part, (back, size) in enumerate(((back_p, 16), (back_q, 8))):
        sent = back.at[pl.ds(0, (PEERS - 1) * size)]
        pltpu.make_async_copy(sent, sent, ret_send.at[part]).wait()
        for i in range(LAYERS):
            gone = send.at[part, i] if i else send.at[part, 0, pl.ds(0, PEERS - 1)]
            pltpu.make_async_copy(gone, gone, fwd_send.at[part]).wait()
    @pl.when(k == 1)
    def _():
        pltpu.make_async_copy(three, three, swap_send).wait()

    for stage in range(3):
        bond_wait(stage, bond_send)


def unpack_kernel(lesser, base, back_q, ret, les, out, sems):
    lesser_copy = pltpu.make_async_copy(lesser, les.at[0, 0], sems.at[LAYERS])
    lesser_copy.start()
    rows = lax.broadcasted_iota(jnp.int32, (N, N), 0)
    cols = lax.broadcasted_iota(jnp.int32, (N, N), 1)
    upper = rows < cols
    off = rows != cols
    zero = jnp.zeros((N, N), F32)
    copies = [
        pltpu.make_async_copy(out.at[i], ret.at[0, 0, i], sems.at[i]) for i in range(LAYERS)
    ]
    for i in range(LAYERS):
        qmat = gather(back_q, 2, i, 0)
        qt = qmat.T
        out[i, 0] = base[i, 0] + 0.5 * jnp.where(upper, qt, qmat)
        out[i, 1] = base[i, 1] + 0.5 * jnp.where(upper, qmat, jnp.where(off, -qt, zero))
        copies[i].start()
    for copy in copies:
        copy.wait()
    lesser_copy.wait()


def shards(hamiltonian, sigma_prev, coupling, coupling_pattern, phonon_shift, phonon_weight):
    dma = pltpu.SemaphoreType.DMA
    found = pl.pallas_call(
        main_kernel,
        out_shape=(
            pltpu.VMEM((LAYERS, 2, N, N), F32),
            pltpu.VMEM((LAYERS, 2, N, N), F32),
            pltpu.VMEM(((PEERS + 1) * 8, N), F32),
        ),
        in_specs=[pl.BlockSpec(memory_space=pl.ANY)] * 6,
        out_specs=(pl.BlockSpec(memory_space=pltpu.VMEM),) * 3,
        scratch_shapes=[
            pltpu.VMEM((2, N, N), F32),
            pltpu.VMEM((4, 2, N, N), F32),
            pltpu.VMEM((N, N), F32),
            pltpu.VMEM((N, N), jnp.int32),
            pltpu.SMEM((PHONONS,), jnp.int32),
            pltpu.SMEM((PHONONS,), F32),
            pltpu.VMEM((LAYERS, 2, N, N), F32),
            pltpu.VMEM((LAYERS, 2, N, N), F32),
            pltpu.VMEM((LAYERS, N, N), F32),
            pltpu.VMEM((LAYERS + 2, 2, N, N), F32),
            pltpu.VMEM((2, LAYERS, PEERS, 2, N), F32),
            pltpu.VMEM((2, MOMS, ENERGIES, 2, N), F32),
            pltpu.VMEM((MOMS, 4 * ENERGIES + 8, N), F32),
            pltpu.VMEM((MOMS, 2 * ENERGIES + 8, N), F32),
            pltpu.VMEM(((PEERS + 1) * 16, N), F32),
        ]
        + [dma] * 2
        + [dma((3,))] * 2
        + [dma((2,))] * 4
        + [dma((9,))]
        + [pltpu.SemaphoreType.REGULAR] * 4,
        compiler_params=pltpu.CompilerParams(collective_id=0, has_side_effects=True),
        name="selfenergy",
    )(
        hamiltonian[0, 0], sigma_prev[0, 0], coupling[0], coupling_pattern,
        phonon_shift, phonon_weight,
    )
    shape = jax.ShapeDtypeStruct((1, 1, 4, 2, N, N), F32)
    return pl.pallas_call(
        unpack_kernel,
        out_shape=(shape, shape),
        in_specs=[pl.BlockSpec(memory_space=pltpu.VMEM)] * 3,
        out_specs=(pl.BlockSpec(memory_space=pl.ANY),) * 2,
        scratch_shapes=[pltpu.VMEM((LAYERS, 2, N, N), F32), dma((LAYERS + 1,))],
        name="unpack",
    )(*(pltpu.with_memory_space_constraint(value, pltpu.VMEM) for value in found))


def solution(mesh):
    in_specs = (
        P("mom", "len", None, None, None),
        P("mom", "len", "energy", None, None, None),
        P("len", None, None),
        P(),
        P(),
        P(),
    )
    out_specs = (
        P("mom", "len", "energy", None, None, None),
        P("mom", "len", "energy", None, None, None),
    )
    return jax.shard_map(shards, mesh=mesh, in_specs=in_specs, out_specs=out_specs, check_vma=False)
```
